32 devices in a mesh: seq: 8 (over z, x), head: 4 (over y, core).
Axes of the slice: x: 2, y: 2, z: 4, core: 2. Of those that a mesh axis runs over, the one named last changes fastest.
Arguments:
- queries: bfloat16 [9216, 32, 128], P(('seq', 'head')), may hold values from -4 to 4
- key_states: bfloat16 [9216, 4, 128], P(('seq', 'head')), may hold values from -4 to 4
- value_states: bfloat16 [9216, 4, 128], P(('seq', 'head')), may hold values from -6 to 6
- outputs: bfloat16 [9216, 32, 128], P(('seq', 'head')), may hold values from -6 to 6
- output_grad: bfloat16 [9216, 32, 128], P(('seq', 'head')), may hold values from -96 to 96
- logsumexp: float32 [9216, 32], P(('seq', 'head')), may hold values from 6.8 to 7.8
- random_owner: int32 [72, 3], replicated, may hold values from 0 to 7, all different within a row; in each aligned block of 9 rows (0 to 8, 9 to 17, ...) at most 4 rows name the same one
- random_slot: int32 [72, 3], replicated, may hold values from 0 to 8
Outputs:
- query_grad: bfloat16 [9216, 32, 128], P(('seq', 'head'))
- key_grad: bfloat16 [9216, 4, 128], P(('seq', 'head'))
- value_grad: bfloat16 [9216, 4, 128], P(('seq', 'head'))
The draws below stay inside these ranges and needn't reach their ends.
Inputs may be any that keep to these rules, and one draw needn't show every extreme that they name: `random_owner`: each row names 3 different indices. Within the 9 rows of one index of seq (aligned blocks of 9 rows), no index of seq appears more than 4 times, and some index appears exactly 4 times in some block.
All inputs are finite; a program needn't handle non-finite values.
Results may differ from the reference program's by a relative error of at most 0.005.
Values may be sent and summed in bfloat16 or wider, within the bound.
A program may use at most 128 MiB of HBM per device.

```python
import math
import jax
import jax.numpy as jnp
import numpy as np
from jax import lax

QH = 32
KVH = 4
HD = 128
BLK = 128
G = 2
RND = 3
TOKENS = 9216
NB = 72
QB = 9
MOST = 4
N_SEQ = 8


def bounded_field(key, field_shape):
    return jnp.clip(jax.random.normal(key, field_shape, jnp.float32), -4.0, 4.0)


def draw_queries(key, part):
    return bounded_field(jax.random.fold_in(key, 11), (TOKENS, QH, HD)).astype(jnp.bfloat16)


def draw_key_states(key, part):
    return bounded_field(jax.random.fold_in(key, 23), (TOKENS, KVH, HD)).astype(jnp.bfloat16)


def set_ends(array, own_key, smallest, top_value):
    extent = array.shape
    spot = [jax.random.randint(jax.random.fold_in(own_key, axis), (), 0, extent[axis]) for axis in range(len(extent))]
    array = array.at[tuple(spot)].set(smallest)
    longest = extent.index(max(extent))
    spot[longest] = (spot[longest] + 1) % extent[longest]
    return array.at[tuple(spot)].set(top_value)


def block_levels(own_key, dims, cuts, smallest, high):
    level = 1.0
    for dim, blocks in cuts:
        draws = jax.random.uniform(jax.random.fold_in(jax.random.fold_in(own_key, 6), dim), (blocks,), jnp.float32, smallest / len(cuts), high / len(cuts))
        level = level * jnp.repeat(jnp.exp(draws), dims[dim] // blocks).reshape((-1,) + (1,) * (len(dims) - 1 - dim))
    return level


def shared_out(stream_key, own, number, rows, amount, top, most, lean):
    ranking = jax.random.permutation(stream_key, amount)
    heavy_load, ordinary = load_shares(amount, rows * top, most, lean, True), load_shares(amount, rows * top, most, lean, False)
    places = jnp.arange(amount)

    def named(tallies, offset_by):
        used = int((tallies > 0).sum())
        fixed = max(1, used // 4)
        passed = fixed + (places - fixed + offset_by * (used - fixed)) % max(1, amount - fixed)
        return jnp.zeros((amount,), jnp.int32).at[ranking[jnp.where(places < fixed, places, passed)]].set(jnp.asarray(tallies, jnp.int32))

    tallies = jnp.where(number % 4 == 0, named(heavy_load, number // 4), named(ordinary, number - number // 4 - 1))
    mixed = jax.random.permutation(jax.random.fold_in(own, 3), amount)
    donor, sink = mixed[0:amount // 2 * 2:2], mixed[1:amount // 2 * 2:2]
    slack = jnp.minimum(tallies[donor] - 1, most - tallies[sink]) // 2
    slack = jnp.where((donor == ranking[0]) | (sink == ranking[0]) | (tallies[sink] == 0), 0, jnp.maximum(slack, 0))
    passed = jax.random.randint(jax.random.fold_in(own, 4), (amount // 2,), 0, 1 << 20) % (slack + 1)
    tallies = tallies.at[donor].add(-passed).at[sink].add(passed)
    members = jnp.searchsorted(jnp.cumsum(tallies), jnp.arange(rows * top), side="right").astype(jnp.int32)
    grid = members.reshape(top, rows).T
    grid = grid[jax.random.permutation(jax.random.fold_in(own, 1), rows)]
    offset_by = jax.random.randint(jax.random.fold_in(own, 2), (rows, 1), 0, top)
    return jnp.take_along_axis(grid, (jnp.arange(top)[None, :] + offset_by) % top, axis=1)


def load_shares(amount, total, reach, slope, full):
    loads = [(1 << 20) // math.isqrt(standing ** slope) + 1 for standing in range(1, amount + 1)]
    largest = reach if full else min(reach, max(-(-total // amount), total * loads[0] // sum(loads)))
    least = 1 if total - largest >= amount - 1 else 0
    counts, spare = [largest] + [least] * (amount - 1), total - largest - least * (amount - 1)
    while spare > 0:
        free = [i for i in range(1, amount) if counts[i] < largest] or [i for i in range(1, amount) if counts[i] < reach]
        mass, left = sum([loads[i] for i in free]), spare
        for i in free:
            addition = min(reach - counts[i], max(1, left * loads[i] // mass), spare)
            counts[i] = counts[i] + addition
            spare = spare - addition
    return np.array(counts)


def noise(own_key, shape, deviation, bound, pieces=(), kind=jnp.bfloat16):
    result = jax.random.normal(own_key, shape, jnp.float32) * deviation
    if len(pieces) > 0:
        result = block_levels(own_key, shape, pieces, -0.22, 0.18) * result
    return jnp.clip(result, min=-bound, max=bound).astype(kind)


def setup_inputs(seed: int = 0) -> dict:
    seeds = jax.random.split(jax.random.key(seed), 9)
    queries = draw_queries(jax.random.fold_in(seeds[8], 71), 0)
    key_states = draw_key_states(jax.random.fold_in(seeds[8], 71), 0)
    value_states = noise(seeds[2], (TOKENS, KVH, HD), 1.0, 6.0, ((0, 32),))
    outputs = noise(seeds[3], (TOKENS, QH, HD), 1.0, 6.0, ((0, 32),))
    output_grad = noise(seeds[4], (TOKENS, QH, HD), 16.0, 96.0, ((0, 32),))
    logsumexp = jnp.clip(6.8 + 1.0 * jax.random.uniform(seeds[5], (TOKENS, QH), jnp.float32) ** block_levels(seeds[5], (TOKENS, QH), ((0, 32),), -0.2, 0.2), 6.8, 7.8)
    random_owner_keys = jax.random.split(jax.random.fold_in(seeds[6], 1), NB // QB)
    random_owner_turns = jax.random.permutation(jax.random.fold_in(seeds[6], 3), NB // QB)
    random_owner = jax.vmap(lambda own, number: shared_out(jax.random.fold_in(seeds[6], 2), own, number, QB, N_SEQ, RND, MOST, 2))(random_owner_keys, random_owner_turns).reshape((NB, RND))
    random_slot = set_ends(jax.random.randint(seeds[7], (NB, RND), 0, QB), jax.random.fold_in(seeds[7], 1), 0, QB - 1).astype(jnp.int32)
    return dict(queries=queries, key_states=key_states, value_states=value_states, outputs=outputs, output_grad=output_grad, logsumexp=logsumexp, random_owner=random_owner, random_slot=random_slot)


def narrow_value(values):
    return lax.optimization_barrier(values.astype(jnp.bfloat16)).astype(values.dtype)


def block_lists(block_id, random_owner, random_slot):
    global_ids = jnp.arange(G, dtype=jnp.int32)
    window_ids = block_id + jnp.arange(-1, 2, dtype=jnp.int32)
    random_ids = (random_owner[block_id] * QB + random_slot[block_id]).astype(jnp.int32)
    window_ok = (window_ids >= G) & (window_ids <= NB - 1)
    random_ok = (random_ids >= G) & (jnp.abs(random_ids - block_id) >= 2)
    validity = jnp.concatenate([jnp.ones((G,), jnp.float32), window_ok.astype(jnp.float32), random_ok.astype(jnp.float32)])
    indices = jnp.clip(jnp.concatenate([global_ids, window_ids, random_ids]), 0, NB - 1).astype(jnp.int32)
    return indices, validity


def block_grads(query_block, grad_block, logsum_block, delta_block, key_blocks, value_blocks, validity):
    scaling = 1.0 / (HD ** 0.5)
    scores = jnp.einsum("ighd,mjgd->mghij", query_block, key_blocks) * scaling
    weights = jnp.exp(scores - jnp.transpose(logsum_block, (1, 2, 0))[None, :, :, :, None]) * validity[:, None, None, None, None]
    weights_rounded = narrow_value(weights)
    weight_grad = jnp.einsum("ighd,mjgd->mghij", grad_block, value_blocks)
    score_grad = narrow_value(weights * (weight_grad - jnp.transpose(delta_block, (1, 2, 0))[None, :, :, :, None]))
    query_part = jnp.einsum("mghij,mjgd->ighd", score_grad, key_blocks) * scaling
    key_part = jnp.einsum("mghij,ighd->mjgd", score_grad, query_block) * scaling
    value_part = jnp.einsum("mghij,ighd->mjgd", weights_rounded, grad_block)
    return query_part, jnp.stack([key_part, value_part], axis=2)


def reference(queries, key_states, value_states, outputs, output_grad, logsumexp, random_owner, random_slot):
    group = QH // KVH
    query_full = queries.astype(jnp.float32).reshape(NB, BLK, KVH, group, HD)
    grad_full = output_grad.astype(jnp.float32).reshape(NB, BLK, KVH, group, HD)
    row_delta = jnp.sum(output_grad.astype(jnp.float32) * outputs.astype(jnp.float32), axis=-1)
    delta_blocks = row_delta.reshape(NB, BLK, KVH, group)
    logsum_blocks = logsumexp.reshape(NB, BLK, KVH, group)
    kv_blocks = jnp.stack([key_states, value_states], axis=1).astype(jnp.float32).reshape(NB, BLK, 2, KVH, HD)

    def advance(carry, block_id):
        indices, validity = block_lists(block_id, random_owner, random_slot)
        chosen = kv_blocks[indices]
        query_part, kv_part = block_grads(query_full[block_id], grad_full[block_id], logsum_blocks[block_id], delta_blocks[block_id], chosen[:, :, 0], chosen[:, :, 1], validity)
        carry = carry.at[indices].add(kv_part)
        return carry, query_part

    initial = jnp.zeros((NB, BLK, 2, KVH, HD), jnp.float32)
    kv_grad, query_parts = lax.scan(advance, initial, jnp.arange(NB, dtype=jnp.int32))
    query_grad = query_parts.reshape(TOKENS, QH, HD).astype(jnp.bfloat16)
    key_grad = kv_grad[:, :, 0].reshape(TOKENS, KVH, HD).astype(jnp.bfloat16)
    value_grad = kv_grad[:, :, 1].reshape(TOKENS, KVH, HD).astype(jnp.bfloat16)
    return (query_grad, key_grad, value_grad)
```

```python
import functools
import math

import jax
import jax.numpy as jnp
from jax import lax
from jax.experimental import pallas as pl
from jax.experimental.pallas import tpu as pltpu
from jax.sharding import PartitionSpec as P

HD = 128
BLK = 128
G = 2
RND = 3
MESH = pl.DeviceIdType.MESH
F32 = jnp.float32
BF16 = jnp.bfloat16
LOG2E = math.log2(math.e)


def greet(n_seq, n_head, seq, head):
    barrier = pltpu.get_barrier_semaphore()

    def to_head(d, c):
        pl.semaphore_signal(
            barrier, inc=1, device_id={"head": lax.rem(head + d, n_head)}, device_id_type=MESH
        )
        return c

    def to_seq(d, c):
        pl.semaphore_signal(
            barrier, inc=1, device_id={"seq": lax.rem(seq + d, n_seq)}, device_id_type=MESH
        )
        return c

    lax.fori_loop(1, n_head, to_head, 0)
    lax.fori_loop(1, n_seq, to_seq, 0)
    pl.semaphore_wait(barrier, n_head + n_seq - 2)


def remote(src, dst, send, recv, **where):
    return pltpu.make_async_remote_copy(
        src_ref=src,
        dst_ref=dst,
        send_sem=send,
        recv_sem=recv,
        device_id=where,
        device_id_type=MESH,
    )


def loop(low, high, body):
    def run(i, c):
        body(i)
        return c

    lax.fori_loop(low, high, run, 0)


def dot(a, b, ca, cb):
    return lax.dot_general(a, b, (((ca,), (cb,)), ((), ())), preferred_element_type=F32)


def pair_grads(k, v, shifts, q, g, delta, scaling):
    scores = dot(k, q, 1, 1) * (scaling * LOG2E)
    weights = jnp.concatenate(
        [jnp.exp2(scores[i * BLK : (i + 1) * BLK] - shift) for i, shift in enumerate(shifts)],
        axis=0,
    )
    score_grad = (weights * (dot(v, g, 1, 1) - delta)).astype(BF16)
    dv = dot(weights.astype(BF16), g, 1, 0)
    dk = dot(score_grad, q, 1, 0) * scaling
    return dk, dv, dot(k, score_grad, 0, 0)


def arrival_order(n_head, toks, blocks, pieces):
    size = toks // pieces
    stages = []
    for b in range(blocks):
        stage = -1
        for part in range(b * BLK // size, (b * BLK + BLK - 1) // size + 1):
            if part // pieces >= n_head // 2:
                stage = max(stage, part % pieces)
        stages.append((stage, b))
    return sorted(stages)


def tables(n_seq, most, blocks, seq, owner, slot, pick, pos, back):
    entries = [(b, j) for b in range(blocks) for j in range(RND)]
    mine = [owner[seq * blocks + b, j] for b, j in entries]
    for e, own in enumerate(mine):
        rank = jnp.int32(0)
        for other in mine[:e]:
            rank = rank + jnp.where(other == own, 1, 0)
        pos[e] = own * most + rank

    def scan(names, values, wanted, table, at, empty):
        count = jnp.int32(0)
        found = [jnp.int32(empty)] * most
        for name, value in zip(names, values):
            hit = name == wanted
            for m in range(most):
                found[m] = jnp.where(jnp.logical_and(hit, count == m), value, found[m])
            count = count + jnp.where(hit, 1, 0)
        for m in range(most):
            table[at * most + m] = found[m]

    def asked(p):
        names = [owner[p * blocks + b, j] for b, j in entries]
        values = [slot[p * blocks + b, j] for b, j in entries]
        scan(names, values, seq, pick, p, -1)

    def answered(p):
        names = [owner[seq * blocks + b, j] for b, j in entries]
        scan(names, [jnp.int32(e) for e in range(len(entries))], p, back, p, 0)

    loop(0, n_seq, asked)
    loop(0, n_seq, answered)


def fused(
    n_seq, n_head, most, blocks, pieces,
    owner, slot, q_in, g_in, o_in, kv_in, lse_in,
    dq_out, kv_out,
    pick, pos, back,
    g_own, o_own, delta_own,
    q_all, g_all, lse_all, delta_all, kv_ext, glob, rand, picked, held, acc, gacc, dq_acc, dq_all,
    rpart, rback, halo_part, halo, gpart, gall, kv_sum,
    ls, os, ks, kr, ts, tr, qs, qr, ds, dr, es, er,
    ss, sr, ns, nr, hs, hr, gs, gr, ps, pr, rs, rr,
):
    seq, head = lax.axis_index("seq"), lax.axis_index("head")
    toks = kv_in.shape[2]
    group = q_in.shape[1] // n_head
    rows = toks * group
    span = n_head * toks
    lines = rows // 128
    step = BLK * group
    half = n_head // 2
    size = toks // pieces
    scaling = 1.0 / HD**0.5
    turn = head // half
    far_half = range(half, n_head)
    plan = arrival_order(n_head, toks, blocks, pieces)

    def partner(d):
        base = lax.rem(head + 2 * (d // 2), n_head)
        return base + (1 - 2 * lax.rem(base, 2)) if d % 2 else base

    sends = list(range(2, n_head)) + [1]
    here = pl.ds(pl.multiple_of(head * toks, toks), toks)
    kv_rows = pl.ds(pl.multiple_of(BLK + head * toks, 32), toks)
    line_rows = pl.ds(head * lines, lines)

    def heads_of(ref, peer):
        return ref.at[:, pl.ds(pl.multiple_of(peer * group, group), group), :]

    own = [
        pltpu.make_async_copy(kv_in.at[head, 0], kv_ext.at[0, kv_rows, :], ls.at[0]),
        pltpu.make_async_copy(kv_in.at[head, 1], kv_ext.at[1, kv_rows, :], ls.at[1]),
        pltpu.make_async_copy(lse_in.at[head], lse_all.at[line_rows], ls.at[2]),
        pltpu.make_async_copy(heads_of(q_in, head), q_all.at[here], ls.at[3]),
        pltpu.make_async_copy(heads_of(g_in, head), g_all.at[here], ls.at[4]),
    ]
    taken = [
        pltpu.make_async_copy(heads_of(src, p), dst.at[p], os.at[i, p])
        for p in range(n_head)
        for i, (src, dst) in enumerate(((g_in, g_own), (o_in, o_own)))
    ]
    for copy in taken + own:
        copy.start()

    greet(n_seq, n_head, seq, head)

    def kv_head(part, d):
        peer = partner(d)
        return remote(
            kv_in.at[peer, part], kv_ext.at[part, kv_rows, :], ks.at[part, d], kr.at[part, d], head=peer
        )

    def line_head(kind, d):
        peer = partner(d)
        src, dst = ((lse_in, lse_all), (delta_own, delta_all))[kind]
        return remote(src.at[peer], dst.at[line_rows], ts.at[kind, d], tr.at[kind, d], head=peer)

    def mirrored(side, i, n):
        return i + side * (n - 1 - 2 * i)

    def piece_send(kind, d, i):
        peer = partner(d)
        side = peer // half
        off = mirrored(side, i, pieces) * size
        src = (q_in, g_in)[kind].at[
            pl.ds(off, size), pl.ds(pl.multiple_of(peer * group, group), group), :
        ]
        dst = (q_all, g_all)[kind].at[pl.ds(head * toks + off, size)]
        return remote(
            src, dst, qs.at[kind, d, i], qr.at[kind, mirrored(side, head, n_head), i], head=peer
        )

    def piece_wait(kind, v, i):
        off = mirrored(turn, v, n_head) * toks + mirrored(turn, i, pieces) * size
        dst = (q_all, g_all)[kind].at[pl.ds(off, size)]
        remote(dst, dst, qs.at[kind, 0, i], qr.at[kind, v, i], head=partner(1)).wait_recv()

    for part in range(2):
        for d in sends:
            kv_head(part, d).start()
    for d in sends:
        line_head(0, d).start()
    for kind in range(2):
        for i in range(pieces):
            piece_send(kind, 1, i).start()

    for copy in taken:
        copy.wait()
    ones = jnp.ones((HD, 128), BF16)
    eye = (
        lax.broadcasted_iota(jnp.int32, (128, 128), 0)
        == lax.broadcasted_iota(jnp.int32, (128, 128), 1)
    ).astype(F32)
    cut = 32
    flat = cut * group
    for p in range(n_head):
        def row_delta(c):
            at = pl.ds(pl.multiple_of(c * cut, cut), cut)
            full = g_own[p, at].reshape(flat, HD).astype(F32) * o_own[p, at].reshape(flat, HD).astype(F32)
            high = full.astype(BF16)
            low = (full - high.astype(F32)).astype(BF16)
            sums = dot(high, ones, 1, 0) + dot(low, ones, 1, 0)
            for r in range(flat // 128):
                line = jnp.sum(sums[r * 128 : (r + 1) * 128] * eye, axis=0, keepdims=True)
                delta_own[p, c * (flat // 128) + r] = line

        loop(0, toks // cut, row_delta)
    delta_all[line_rows] = delta_own[head]
    for d in sends:
        line_head(1, d).start()
    for i in range(pieces):
        for kind in range(2):
            for d in range(2, n_head):
                piece_send(kind, d, i).start()
    tables(n_seq, most, blocks, seq, owner, slot, pick, pos, back)

    up, down = lax.rem(seq + 1, n_seq), lax.rem(seq + n_seq - 1, n_seq)

    def to_up(part):
        return remote(
            kv_ext.at[part, pl.ds(span, BLK), :], kv_ext.at[part, pl.ds(0, BLK), :],
            ns.at[part, 0], nr.at[part, 0], seq=up,
        )

    def to_down(part):
        return remote(
            kv_ext.at[part, pl.ds(BLK, BLK), :], kv_ext.at[part, pl.ds(BLK + span, BLK), :],
            ns.at[part, 1], nr.at[part, 1], seq=down,
        )

    def slots_of(peer):
        return pl.ds(peer * most, most)

    def rand_copy(part, d):
        peer = lax.rem(seq + d, n_seq)
        return remote(
            picked.at[part, slots_of(peer)], rand.at[part, slots_of(seq)],
            ss.at[part, d], sr.at[part, d], seq=peer,
        )

    def glob_copy(part, d):
        return remote(
            kv_ext.at[part, pl.ds(BLK, G * BLK), :], glob.at[part], gs.at[part, d], gr.at[part], seq=d
        )

    for part in range(2):
        own[part].wait()
        for d in range(1, n_head):
            kv_head(part, d).wait_recv()
        for block in range(blocks):
            held[part, block] = kv_ext[part, (block + 1) * BLK : (block + 2) * BLK, :]
        def fill(i):
            picked[part, i] = held[part, jnp.maximum(pick[i], 0)]

        loop(0, n_seq * most, fill)
        to_up(part).start()
        to_down(part).start()

        @pl.when(seq == 0)
        def _():
            loop(1, n_seq, lambda d: glob_copy(part, d).start())
            glob[part] = kv_ext[part, BLK : BLK + G * BLK, :]

        loop(1, n_seq, lambda d: rand_copy(part, d).start())
        rand[part, slots_of(seq)] = picked[part, slots_of(seq)]

    acc[...] = jnp.zeros_like(acc)
    gacc[...] = jnp.zeros_like(gacc)
    for part in range(2):
        to_up(part).wait()
        to_down(part).wait()

    @pl.when(seq > 0)
    def _():
        for part in range(2):
            glob_copy(part, 0).wait_recv()

    for copy in own[2:]:
        copy.wait()
    for kind in range(2):
        for d in range(1, n_head):
            line_head(kind, d).wait_recv()
        for k in range(1, half):
            v = lax.rem(mirrored(turn, head, n_head) + k, half)
            for i in range(pieces):
                piece_wait(kind, v, i)

    def landed(i):
        for kind in range(2):
            for v in far_half:
                piece_wait(kind, v, i)

    def block_at(i):
        b = jnp.int32(plan[0][1])
        for k in range(1, blocks):
            b = jnp.where(i == k, plan[k][1], b)
        return mirrored(turn, b, blocks)

    def operands(b):
        spot = pl.ds(pl.multiple_of(b * BLK, BLK), BLK)
        per = step // 128

        def lanes(ref):
            tile = ref[pl.ds(b * per, per)]
            return jnp.concatenate([tile[r] for r in range(per)], axis=1)

        flat = (step, HD)
        return q_all[spot].reshape(flat), g_all[spot].reshape(flat), lanes(lse_all) * LOG2E, lanes(delta_all)

    def hidden(okay):
        return jnp.where(okay, 0.0, 1e30).astype(F32)

    def near(i, fresh):
        b = block_at(i)
        q, g, lse, delta = operands(b)
        at = pl.multiple_of(b * BLK, BLK)
        win = pl.ds(at, 3 * BLK)
        dk, dv, dq = pair_grads(glob[0], glob[1], [lse] * G, q, g, delta, scaling)
        gacc[0] += dk
        gacc[1] += dv
        block = seq * blocks + b
        shifts = []
        for j in range(-1, 2):
            okay = jnp.logical_and(block + j >= G, block + j <= n_seq * blocks - 1)
            shifts.append(lse + hidden(okay))
        dk, dv, more = pair_grads(kv_ext[0, win, :], kv_ext[1, win, :], shifts, q, g, delta, scaling)
        acc[0, win, :] += dk
        acc[1, win, :] += dv
        if fresh:
            dq_acc[b] = dq + more
        else:
            total = dq_acc[b] + dq + more
            dq_all[pl.ds(at, BLK)] = (total.T * scaling).astype(BF16).reshape(BLK, group, HD)

    def far(i, fresh):
        b = block_at(i)
        q, g, lse, delta = operands(b)
        at = pl.multiple_of(b * BLK, BLK)
        block = seq * blocks + b
        k = jnp.concatenate([rand[0, pos[b * RND + j]] for j in range(RND)], axis=0)
        v = jnp.concatenate([rand[1, pos[b * RND + j]] for j in range(RND)], axis=0)
        shifts = []
        for j in range(RND):
            other = owner[block, j] * blocks + slot[block, j]
            okay = jnp.logical_and(other >= G, jnp.abs(other - block) >= 2)
            shifts.append(lse + hidden(okay))
        dk, dv, dq = pair_grads(k, v, shifts, q, g, delta, scaling)
        for j in range(RND):
            rpart[0, b * RND + j] = dk[j * BLK : (j + 1) * BLK].astype(BF16)
            rpart[1, b * RND + j] = dv[j * BLK : (j + 1) * BLK].astype(BF16)
        if fresh:
            dq_acc[b] = dq
        else:
            total = dq_acc[b] + dq
            dq_all[pl.ds(at, BLK)] = (total.T * scaling).astype(BF16).reshape(BLK, group, HD)

    last = pieces - 1
    early = sum(stage < last for stage, _ in plan)
    firsts = {}
    for i, (stage, _) in enumerate(plan):
        for s in range(stage + 1):
            firsts.setdefault(s, i)

    def near_early(i):
        for s in range(last):
            if s in firsts and firsts[s] < early:
                @pl.when(i == firsts[s])
                def _():
                    landed(s)

        near(i, True)

    loop(0, early, near_early)
    for s in range(last):
        if s not in firsts or firsts[s] >= early:
            landed(s)
    for part in range(2):
        loop(1, n_seq, lambda d: rand_copy(part, d).wait())
    loop(0, early, lambda i: far(i, False))
    landed(last)
    loop(early, blocks, lambda i: far(i, True))

    def back_copy(part, d):
        peer = lax.rem(seq + d, n_seq)
        return remote(
            picked.at[part, slots_of(peer)], rback.at[part, slots_of(seq)],
            rs.at[part, d], rr.at[part, d], seq=peer,
        )

    def gather(part):
        def move(i):
            picked[part, i] = rpart[part, back[i]]

        loop(0, n_seq * most, move)

    gather(1)
    loop(1, n_seq, lambda d: back_copy(1, d).start())
    loop(early, blocks, lambda i: near(i, False))

    halo_part[0] = acc[:, 0:BLK, :].astype(BF16)
    halo_part[1] = acc[:, BLK + span :, :].astype(BF16)
    gpart[...] = gacc[...].astype(BF16)

    def dq_copy(d):
        peer = partner(d)
        src = dq_all.at[pl.ds(pl.multiple_of(peer * toks, toks), toks)]
        return remote(src, heads_of(dq_out, head), ds.at[d], dr.at[d], head=peer)

    def kv_copy(part, d):
        peer = partner(d)
        src = kv_sum.at[part, pl.ds(pl.multiple_of(peer * toks, 32), toks), :]
        return remote(src, kv_out.at[head, part], es.at[part, d], er.at[part, d], head=peer)

    def part_copy():
        return remote(gpart, gall.at[seq], ps.at[0], pr.at[seq], seq=0)

    down_grad = remote(halo_part.at[0], halo.at[0], hs.at[0], hr.at[0], seq=down)
    up_grad = remote(halo_part.at[1], halo.at[1], hs.at[1], hr.at[1], seq=up)
    down_grad.start()
    up_grad.start()

    @pl.when(seq > 0)
    def _():
        part_copy().start()

    gather(0)
    loop(1, n_seq, lambda d: back_copy(0, d).start())
    own_dq = pltpu.make_async_copy(dq_all.at[here], heads_of(dq_out, head), ls.at[5])
    for d in sends:
        dq_copy(d).start()
    own_dq.start()
    for part in range(2):
        rback[part, slots_of(seq)] = picked[part, slots_of(seq)]

    for d in range(1, n_head):
        for kind in range(2):
            kv_head(kind, d).wait_send()
            line_head(kind, d).wait_send()
            for i in range(pieces):
                piece_send(kind, d, i).wait_send()

    def absorb(part, d):
        base = lax.rem(seq + n_seq - d, n_seq) * most

        def block_sum(block):
            over = pl.ds(pl.multiple_of(block * BLK + BLK, BLK), BLK)
            value = acc[part, over, :]
            for m in range(most):
                share = jnp.where(pick[base + m] == block, 1.0, 0.0).astype(F32)
                value = value + share * rback[part, base + m].astype(F32)
            acc[part, over, :] = value

        loop(0, blocks, block_sum)

    absorb(1, 0)
    absorb(0, 0)

    @pl.when(seq == 0)
    def _():
        for part in range(2):
            loop(1, n_seq, lambda d: glob_copy(part, d).wait_send())
        gall[0] = gpart[...]

    for part in (1, 0):
        def take(d):
            back_copy(part, d).wait()
            absorb(part, d)

        loop(1, n_seq, take)
        if part:
            @pl.when(seq == 0)
            def _():
                def arrive(d):
                    remote(gpart, gall.at[d], ps.at[0], pr.at[d], seq=0).wait_recv()

                loop(1, n_seq, arrive)

                def add(d):
                    gacc[...] += gall[d].astype(F32)

                loop(1, n_seq, add)
                acc[:, BLK : BLK + G * BLK, :] += gacc[...]

            @pl.when(seq > 0)
            def _():
                part_copy().wait_send()

            down_grad.wait()
            up_grad.wait()
            acc[:, BLK : 2 * BLK, :] += halo[1].astype(F32)
            acc[:, span : span + BLK, :] += halo[0].astype(F32)
        kv_sum[part] = acc[part, BLK : BLK + span, :].astype(BF16)
        for d in sends:
            kv_copy(part, d).start()
        kv_out[head, part] = kv_sum[part, pl.ds(pl.multiple_of(head * toks, 32), toks), :]
    own_dq.wait()
    for d in range(1, n_head):
        dq_copy(d).wait()
    for part in range(2):
        for d in range(1, n_head):
            kv_copy(part, d).wait()


def per_device(
    n_seq, n_head,
    queries, key_states, value_states, outputs, output_grad, logsumexp, random_owner, random_slot,
):
    toks, heads, _ = queries.shape
    group = heads // n_head
    rows = toks * group
    span = toks * n_head
    blocks = span // BLK
    per_row = blocks * RND
    most = max(1, (per_row + n_seq - 1) // n_seq)
    pieces = 3 if toks % 3 == 0 else 1
    vmem = pl.BlockSpec(memory_space=pltpu.VMEM)
    smem = pl.BlockSpec(memory_space=pltpu.SMEM)
    hbm = pl.BlockSpec(memory_space=pl.ANY)
    dma = pltpu.SemaphoreType.DMA

    lse = jnp.transpose(logsumexp.reshape(toks, n_head, group), (1, 0, 2))
    lse = lse.reshape(n_head, rows // 128, 1, 128)
    kv = jnp.transpose(jnp.stack([key_states, value_states]), (2, 0, 1, 3))

    slots = n_seq * most
    step = BLK * group
    query_grad, kv_all = pl.pallas_call(
        functools.partial(fused, n_seq, n_head, most, blocks, pieces),
        out_shape=[
            jax.ShapeDtypeStruct((toks, heads, HD), BF16),
            jax.ShapeDtypeStruct((n_head, 2, toks, HD), BF16),
        ],
        in_specs=[smem, smem, hbm, hbm, hbm, vmem, vmem],
        out_specs=[hbm, vmem],
        scratch_shapes=[
            pltpu.SMEM((slots,), jnp.int32),
            pltpu.SMEM((per_row,), jnp.int32),
            pltpu.SMEM((slots,), jnp.int32),
            pltpu.VMEM((n_head, toks, group, HD), BF16),
            pltpu.VMEM((n_head, toks, group, HD), BF16),
            pltpu.VMEM((n_head, rows // 128, 1, 128), F32),
            pltpu.VMEM((span, group, HD), BF16),
            pltpu.VMEM((span, group, HD), BF16),
            pltpu.VMEM((n_head * rows // 128, 1, 128), F32),
            pltpu.VMEM((n_head * rows // 128, 1, 128), F32),
            pltpu.VMEM((2, span + 2 * BLK, HD), BF16),
            pltpu.VMEM((2, G * BLK, HD), BF16),
            pltpu.VMEM((2, slots, BLK, HD), BF16),
            pltpu.VMEM((2, slots, BLK, HD), BF16),
            pltpu.VMEM((2, blocks, BLK, HD), BF16),
            pltpu.VMEM((2, span + 2 * BLK, HD), F32),
            pltpu.VMEM((2, G * BLK, HD), F32),
            pltpu.VMEM((blocks, HD, step), F32),
            pltpu.VMEM((span, group, HD), BF16),
            pltpu.VMEM((2, per_row, BLK, HD), BF16),
            pltpu.VMEM((2, slots, BLK, HD), BF16),
            pltpu.VMEM((2, 2, BLK, HD), BF16),
            pltpu.VMEM((2, 2, BLK, HD), BF16),
            pltpu.VMEM((2, G * BLK, HD), BF16),
            pltpu.VMEM((n_seq, 2, G * BLK, HD), BF16),
            pltpu.VMEM((2, span, HD), BF16),
            dma((6,)), dma((2, n_head)), dma((2, n_head)), dma((2, n_head)),
            dma((2, n_head)), dma((2, n_head)),
            dma((2, n_head, pieces)), dma((2, n_head, pieces)),
            dma((n_head,)), dma((n_head,)), dma((2, n_head)), dma((2, n_head)),
            dma((2, n_seq)), dma((2, n_seq)), dma((2, 2)), dma((2, 2)), dma((2,)), dma((2,)),
            dma((2, n_seq)), dma((2,)), dma((1,)), dma((n_seq,)),
            dma((2, n_seq)), dma((2, n_seq)),
        ],
        compiler_params=pltpu.CompilerParams(
            collective_id=0, has_side_effects=True, vmem_limit_bytes=60 << 20
        ),
        name="fused",
    )(random_owner, random_slot, queries, output_grad, outputs, kv, lse)

    key_grad = jnp.transpose(kv_all[:, 0], (1, 0, 2))
    value_grad = jnp.transpose(kv_all[:, 1], (1, 0, 2))
    return query_grad, key_grad, value_grad


def solution(mesh):
    wide = P(("seq", "head"), None, None)
    return jax.shard_map(
        functools.partial(per_device, mesh.shape["seq"], mesh.shape["head"]),
        mesh=mesh,
        in_specs=(wide, wide, wide, wide, wide, P(("seq", "head"), None), P(), P()),
        out_specs=(wide, wide, wide),
        check_vma=False,
    )
```

```python
import functools
import math

import jax
import jax.numpy as jnp
from jax import lax
from jax.experimental import pallas as pl
from jax.experimental.pallas import tpu as pltpu
from jax.sharding import PartitionSpec as P

HD = 128
BLK = 128
G = 2
RND = 3
MESH = pl.DeviceIdType.MESH
F32 = jnp.float32
BF16 = jnp.bfloat16
LOG2E = math.log2(math.e)


def greet(n_seq, n_head, seq, head):
    barrier = pltpu.get_barrier_semaphore()

    def to_head(d, c):
        pl.semaphore_signal(
            barrier, inc=1, device_id={"head": lax.rem(head + d, n_head)}, device_id_type=MESH
        )
        return c

    def to_seq(d, c):
        pl.semaphore_signal(
            barrier, inc=1, device_id={"seq": lax.rem(seq + d, n_seq)}, device_id_type=MESH
        )
        return c

    lax.fori_loop(1, n_head, to_head, 0)
    lax.fori_loop(1, n_seq, to_seq, 0)
    pl.semaphore_wait(barrier, n_head + n_seq - 2)


def remote(src, dst, send, recv, **where):
    return pltpu.make_async_remote_copy(
        src_ref=src,
        dst_ref=dst,
        send_sem=send,
        recv_sem=recv,
        device_id=where,
        device_id_type=MESH,
    )


def loop(low, high, body):
    def run(i, c):
        body(i)
        return c

    lax.fori_loop(low, high, run, 0)


def dot(a, b, ca, cb):
    return lax.dot_general(a, b, (((ca,), (cb,)), ((), ())), preferred_element_type=F32)


def pair_grads(k, v, shifts, q, g, delta, scaling):
    scores = dot(k, q, 1, 1) * (scaling * LOG2E)
    weights = jnp.concatenate(
        [jnp.exp2(scores[i * BLK : (i + 1) * BLK] - shift) for i, shift in enumerate(shifts)],
        axis=0,
    )
    score_grad = (weights * (dot(v, g, 1, 1) - delta)).astype(BF16)
    dv = dot(weights.astype(BF16), g, 1, 0)
    dk = dot(score_grad, q, 1, 0) * scaling
    return dk, dv, dot(k, score_grad, 0, 0)


def arrival_order(n_head, toks, blocks, pieces):
    size = toks // pieces
    stages = []
    for b in range(blocks):
        stage = -1
        for part in range(b * BLK // size, (b * BLK + BLK - 1) // size + 1):
            if part // pieces >= n_head // 2:
                stage = max(stage, part % pieces)
        stages.append((stage, b))
    return sorted(stages)


def tables(n_seq, most, blocks, seq, owner, slot, pick, pos, back):
    entries = [(b, j) for b in range(blocks) for j in range(RND)]
    mine = [owner[j, seq * blocks + b] for b, j in entries]
    for e, own in enumerate(mine):
        rank = jnp.int32(0)
        for other in mine[:e]:
            rank = rank + jnp.where(other == own, 1, 0)
        pos[e] = own * most + rank

    def scan(names, values, wanted, table, at, empty):
        count = jnp.int32(0)
        found = [jnp.int32(empty)] * most
        for name, value in zip(names, values):
            hit = name == wanted
            for m in range(most):
                found[m] = jnp.where(jnp.logical_and(hit, count == m), value, found[m])
            count = count + jnp.where(hit, 1, 0)
        for m in range(most):
            table[at * most + m] = found[m]

    def asked(p):
        names = [owner[j, p * blocks + b] for b, j in entries]
        values = [slot[j, p * blocks + b] for b, j in entries]
        scan(names, values, seq, pick, p, -1)

    def answered(p):
        names = [owner[j, seq * blocks + b] for b, j in entries]
        scan(names, [jnp.int32(e) for e in range(len(entries))], p, back, p, 0)

    loop(0, n_seq, asked)
    loop(0, n_seq, answered)


def fused(
    n_seq, n_head, most, blocks, pieces,
    owner, slot, q_in, g_in, o_in, kv_in, lse_in,
    dq_out, kv_out,
    pick, pos, back,
    far_weights, g_own, o_own, delta_own,
    q_all, g_all, lse_all, delta_all, kv_ext, glob, rand_k, rand_v, picked, held, acc, gacc, dq_acc, dq_all,
    rpart, rback, halo_part, halo, gpart, gall, kv_sum,
    ls, os, ks, kr, ts, tr, qs, qr, ds, dr, es, er,
    ss, sr, ns, nr, hs, hr, gs, gr, ps, pr, rs, rr,
):
    seq, head = lax.axis_index("seq"), lax.axis_index("head")
    toks = kv_in.shape[2]
    group = q_in.shape[1] // n_head
    rows = toks * group
    span = n_head * toks
    lines = rows // 128
    step = BLK * group
    half = n_head // 2
    size = toks // pieces
    scaling = 1.0 / HD**0.5
    turn = head // half
    far_half = range(half, n_head)
    rand = (rand_k, rand_v)
    plan = arrival_order(n_head, toks, blocks, pieces)

    def partner(d):
        base = lax.rem(head + 2 * (d // 2), n_head)
        return base + (1 - 2 * lax.rem(base, 2)) if d % 2 else base

    sends = list(range(2, n_head)) + [1]
    here = pl.ds(pl.multiple_of(head * toks, toks), toks)
    kv_rows = pl.ds(pl.multiple_of(BLK + head * toks, 32), toks)
    line_rows = pl.ds(head * lines, lines)

    def heads_of(ref, peer):
        return ref.at[:, pl.ds(pl.multiple_of(peer * group, group), group), :]

    own = [
        pltpu.make_async_copy(kv_in.at[head, 0], kv_ext.at[0, kv_rows, :], ls.at[0]),
        pltpu.make_async_copy(kv_in.at[head, 1], kv_ext.at[1, kv_rows, :], ls.at[1]),
        pltpu.make_async_copy(lse_in.at[head], lse_all.at[line_rows], ls.at[2]),
        pltpu.make_async_copy(heads_of(q_in, head), q_all.at[here], ls.at[3]),
        pltpu.make_async_copy(heads_of(g_in, head), g_all.at[here], ls.at[4]),
    ]
    taken = [
        pltpu.make_async_copy(heads_of(src, p), dst.at[p], os.at[i, p])
        for p in range(n_head)
        for i, (src, dst) in enumerate(((g_in, g_own), (o_in, o_own)))
    ]
    for copy in taken + own:
        copy.start()

    greet(n_seq, n_head, seq, head)

    def kv_head(part, d):
        peer = partner(d)
        return remote(
            kv_in.at[peer, part], kv_ext.at[part, kv_rows, :], ks.at[part, d], kr.at[part, d], head=peer
        )

    def line_head(kind, d):
        peer = partner(d)
        src, dst = ((lse_in, lse_all), (delta_own, delta_all))[kind]
        return remote(src.at[peer], dst.at[line_rows], ts.at[kind, d], tr.at[kind, d], head=peer)

    def mirrored(side, i, n):
        return i + side * (n - 1 - 2 * i)

    def piece_send(kind, d, i):
        peer = partner(d)
        side = peer // half
        off = mirrored(side, i, pieces) * size
        src = (q_in, g_in)[kind].at[
            pl.ds(off, size), pl.ds(pl.multiple_of(peer * group, group), group), :
        ]
        dst = (q_all, g_all)[kind].at[pl.ds(head * toks + off, size)]
        return remote(
            src, dst, qs.at[kind, d, i], qr.at[kind, mirrored(side, head, n_head), i], head=peer
        )

    def piece_wait(kind, v, i):
        off = mirrored(turn, v, n_head) * toks + mirrored(turn, i, pieces) * size
        dst = (q_all, g_all)[kind].at[pl.ds(off, size)]
        remote(dst, dst, qs.at[kind, 0, i], qr.at[kind, v, i], head=partner(1)).wait_recv()

    for part in range(2):
        for d in sends:
            kv_head(part, d).start()
    for d in sends:
        line_head(0, d).start()
    for kind in range(2):
        for i in range(pieces):
            piece_send(kind, 1, i).start()
    for kind in range(2):
        for d in range(2, n_head):
            piece_send(kind, d, 0).start()

    tables(n_seq, most, blocks, seq, owner, slot, pick, pos, back)

    up, down = lax.rem(seq + 1, n_seq), lax.rem(seq + n_seq - 1, n_seq)

    def to_up(part):
        return remote(
            kv_ext.at[part, pl.ds(span, BLK), :], kv_ext.at[part, pl.ds(0, BLK), :],
            ns.at[part, 0], nr.at[part, 0], seq=up,
        )

    def to_down(part):
        return remote(
            kv_ext.at[part, pl.ds(BLK, BLK), :], kv_ext.at[part, pl.ds(BLK + span, BLK), :],
            ns.at[part, 1], nr.at[part, 1], seq=down,
        )

    def slots_of(peer):
        return pl.ds(peer * most, most)

    def rand_copy(part, d):
        peer = lax.rem(seq + d, n_seq)
        return remote(
            picked.at[part, slots_of(peer)], rand[part].at[slots_of(seq)],
            ss.at[part, d], sr.at[part, d], seq=peer,
        )

    def glob_copy(part, d):
        return remote(
            kv_ext.at[part, pl.ds(BLK, G * BLK), :], glob.at[part], gs.at[part, d], gr.at[part], seq=d
        )

    for part in range(2):
        own[part].wait()
        for d in range(1, n_head):
            kv_head(part, d).wait_recv()
        for block in range(blocks):
            held[part, block] = kv_ext[part, (block + 1) * BLK : (block + 2) * BLK, :]
        def fill(i):
            picked[part, i] = held[part, jnp.maximum(pick[i], 0)]

        loop(0, n_seq * most, fill)
        to_up(part).start()
        to_down(part).start()

        @pl.when(seq == 0)
        def _():
            loop(1, n_seq, lambda d: glob_copy(part, d).start())
            glob[part] = kv_ext[part, BLK : BLK + G * BLK, :]

        loop(1, n_seq, lambda d: rand_copy(part, d).start())
        rand[part][slots_of(seq)] = picked[part, slots_of(seq)]

    for copy in taken:
        copy.wait()
    ones = jnp.ones((HD, 128), BF16)
    eye = (
        lax.broadcasted_iota(jnp.int32, (128, 128), 0)
        == lax.broadcasted_iota(jnp.int32, (128, 128), 1)
    ).astype(F32)
    cut = 32
    flat = cut * group
    for p in range(n_head):
        def row_delta(c):
            at = pl.ds(pl.multiple_of(c * cut, cut), cut)
            full = g_own[p, at].reshape(flat, HD).astype(F32) * o_own[p, at].reshape(flat, HD).astype(F32)
            high = full.astype(BF16)
            low = (full - high.astype(F32)).astype(BF16)
            sums = dot(high, ones, 1, 0) + dot(low, ones, 1, 0)
            for r in range(flat // 128):
                line = jnp.sum(sums[r * 128 : (r + 1) * 128] * eye, axis=0, keepdims=True)
                delta_own[p, c * (flat // 128) + r] = line

        loop(0, toks // cut, row_delta)
    delta_all[line_rows] = delta_own[head]
    for d in sends:
        line_head(1, d).start()
    for i in range(1, pieces):
        for kind in range(2):
            for d in range(2, n_head):
                piece_send(kind, d, i).start()

    acc[...] = jnp.zeros_like(acc)
    gacc[...] = jnp.zeros_like(gacc)
    for part in range(2):
        to_up(part).wait()
        to_down(part).wait()

    @pl.when(seq > 0)
    def _():
        for part in range(2):
            glob_copy(part, 0).wait_recv()

    for copy in own[2:]:
        copy.wait()
    soon = [1] if half == 2 else list(range(1, n_head))
    for d in range(1, n_head):
        line_head(0, d).wait_recv()
    for d in soon:
        line_head(1, d).wait_recv()
    for kind in range(2):
        for k in range(1, half):
            v = lax.rem(mirrored(turn, head, n_head) + k, half)
            for i in range(pieces):
                piece_wait(kind, v, i)

    def landed(i):
        if i == 0:
            for d in range(1, n_head):
                if d not in soon:
                    line_head(1, d).wait_recv()
        for kind in range(2):
            for v in far_half:
                piece_wait(kind, v, i)

    def block_at(i):
        b = jnp.int32(plan[0][1])
        for k in range(1, blocks):
            b = jnp.where(i == k, plan[k][1], b)
        return mirrored(turn, b, blocks)

    def operands(b):
        spot = pl.ds(pl.multiple_of(b * BLK, BLK), BLK)
        per = step // 128

        def lanes(ref):
            tile = ref[pl.ds(b * per, per)]
            return jnp.concatenate([tile[r] for r in range(per)], axis=1)

        flat = (step, HD)
        return q_all[spot].reshape(flat), g_all[spot].reshape(flat), lanes(lse_all) * LOG2E, lanes(delta_all)

    def hidden(okay):
        return jnp.where(okay, 0.0, 1e30).astype(F32)

    def near(i):
        b = block_at(i)
        q, g, lse, delta = operands(b)
        at = pl.multiple_of(b * BLK, BLK)
        win = pl.ds(at, 3 * BLK)
        dk, dv, dq = pair_grads(glob[0], glob[1], [lse] * G, q, g, delta, scaling)
        gacc[0] += dk
        gacc[1] += dv
        block = seq * blocks + b
        shifts = []
        for j in range(-1, 2):
            okay = jnp.logical_and(block + j >= G, block + j <= n_seq * blocks - 1)
            shifts.append(lse + hidden(okay))
        dk, dv, more = pair_grads(kv_ext[0, win, :], kv_ext[1, win, :], shifts, q, g, delta, scaling)
        acc[0, win, :] += dk
        acc[1, win, :] += dv
        dq_acc[b] = dq + more

    def found(part, b):
        return jnp.concatenate([rand[part][pos[b * RND + j]] for j in range(RND)], axis=0)

    def far_values(i):
        b = block_at(i)
        q, g, lse, _ = operands(b)
        block = seq * blocks + b
        scores = dot(found(0, b), q, 1, 1) * (scaling * LOG2E)
        parts = []
        for j in range(RND):
            other = owner[j, block] * blocks + slot[j, block]
            okay = jnp.logical_and(other >= G, jnp.abs(other - block) >= 2)
            shift = lse + hidden(okay)
            parts.append(jnp.exp2(scores[j * BLK : (j + 1) * BLK] - shift).astype(BF16))
        weights = jnp.concatenate(parts, axis=0)
        far_weights[b] = weights
        dv = dot(weights, g, 1, 0)
        for j in range(RND):
            rpart[1, b * RND + j] = dv[j * BLK : (j + 1) * BLK].astype(BF16)

    def far_keys(i):
        b = block_at(i)
        q, g, _, delta = operands(b)
        at = pl.multiple_of(b * BLK, BLK)
        rise = dot(found(1, b), g, 1, 1) - delta
        score_grad = (far_weights[b].astype(F32) * rise).astype(BF16)
        dk = dot(score_grad, q, 1, 0) * scaling
        for j in range(RND):
            rpart[0, b * RND + j] = dk[j * BLK : (j + 1) * BLK].astype(BF16)
        total = dq_acc[b] + dot(found(0, b), score_grad, 0, 0)
        dq_all[pl.ds(at, BLK)] = (total.T * scaling).astype(BF16).reshape(BLK, group, HD)

    last = pieces - 1
    early = sum(stage < last for stage, _ in plan)
    firsts = {}
    for i, (stage, _) in enumerate(plan):
        for s in range(stage + 1):
            firsts.setdefault(s, i)

    def near_early(i):
        for s in range(last):
            if s in firsts and firsts[s] < early:
                @pl.when(i == firsts[s])
                def _():
                    landed(s)

        near(i)

    loop(0, early, near_early)
    for s in range(last):
        if s not in firsts or firsts[s] >= early:
            landed(s)
    loop(1, n_seq, lambda d: rand_copy(0, d).wait())
    loop(0, early, far_values)
    landed(last)
    loop(early, blocks, far_values)
    loop(1, n_seq, lambda d: rand_copy(1, d).wait_send())

    def back_copy(part, d):
        peer = lax.rem(seq + d, n_seq)
        return remote(
            picked.at[part, slots_of(peer)], rback.at[part, slots_of(seq)],
            rs.at[part, d], rr.at[part, d], seq=peer,
        )

    def gather(part):
        def move(i):
            picked[part, i] = rpart[part, back[i]]

        loop(0, n_seq * most, move)

    gather(1)
    loop(1, n_seq, lambda d: back_copy(1, d).start())
    loop(early, blocks, near)

    halo_part[0] = acc[:, 0:BLK, :].astype(BF16)
    halo_part[1] = acc[:, BLK + span :, :].astype(BF16)
    gpart[...] = gacc[...].astype(BF16)

    def dq_copy(d):
        peer = partner(d)
        src = dq_all.at[pl.ds(pl.multiple_of(peer * toks, toks), toks)]
        return remote(src, heads_of(dq_out, head), ds.at[d], dr.at[d], head=peer)

    def kv_copy(part, d):
        peer = partner(d)
        src = kv_sum.at[part, pl.ds(pl.multiple_of(peer * toks, 32), toks), :]
        return remote(src, kv_out.at[head, part], es.at[part, d], er.at[part, d], head=peer)

    def part_copy():
        return remote(gpart, gall.at[seq], ps.at[0], pr.at[seq], seq=0)

    down_grad = remote(halo_part.at[0], halo.at[0], hs.at[0], hr.at[0], seq=down)
    up_grad = remote(halo_part.at[1], halo.at[1], hs.at[1], hr.at[1], seq=up)
    down_grad.start()
    up_grad.start()

    @pl.when(seq > 0)
    def _():
        part_copy().start()

    loop(1, n_seq, lambda d: rand_copy(1, d).wait_recv())
    loop(0, blocks, far_keys)
    gather(0)
    loop(1, n_seq, lambda d: back_copy(0, d).start())
    own_dq = pltpu.make_async_copy(dq_all.at[here], heads_of(dq_out, head), ls.at[5])
    for d in sends:
        dq_copy(d).start()
    own_dq.start()
    for part in range(2):
        rback[part, slots_of(seq)] = picked[part, slots_of(seq)]

    for d in range(1, n_head):
        for kind in range(2):
            kv_head(kind, d).wait_send()
            line_head(kind, d).wait_send()
            for i in range(pieces):
                piece_send(kind, d, i).wait_send()

    def absorb(part, d):
        base = lax.rem(seq + n_seq - d, n_seq) * most

        def block_sum(block):
            over = pl.ds(pl.multiple_of(block * BLK + BLK, BLK), BLK)
            value = acc[part, over, :]
            for m in range(most):
                share = jnp.where(pick[base + m] == block, 1.0, 0.0).astype(F32)
                value = value + share * rback[part, base + m].astype(F32)
            acc[part, over, :] = value

        loop(0, blocks, block_sum)

    absorb(1, 0)
    absorb(0, 0)

    @pl.when(seq == 0)
    def _():
        for part in range(2):
            loop(1, n_seq, lambda d: glob_copy(part, d).wait_send())
        gall[0] = gpart[...]

    for part in (1, 0):
        def take(d):
            back_copy(part, d).wait()
            absorb(part, d)

        loop(1, n_seq, take)
        if part:
            @pl.when(seq == 0)
            def _():
                def arrive(d):
                    remote(gpart, gall.at[d], ps.at[0], pr.at[d], seq=0).wait_recv()

                loop(1, n_seq, arrive)

                def add(d):
                    gacc[...] += gall[d].astype(F32)

                loop(1, n_seq, add)
                acc[:, BLK : BLK + G * BLK, :] += gacc[...]

            @pl.when(seq > 0)
            def _():
                part_copy().wait_send()

            down_grad.wait()
            up_grad.wait()
            acc[:, BLK : 2 * BLK, :] += halo[1].astype(F32)
            acc[:, span : span + BLK, :] += halo[0].astype(F32)
        kv_sum[part] = acc[part, BLK : BLK + span, :].astype(BF16)
        for d in sends:
            kv_copy(part, d).start()
        kv_out[head, part] = kv_sum[part, pl.ds(pl.multiple_of(head * toks, 32), toks), :]
    own_dq.wait()
    for d in range(1, n_head):
        dq_copy(d).wait()
    for part in range(2):
        for d in range(1, n_head):
            kv_copy(part, d).wait()


def per_device(
    n_seq, n_head,
    queries, key_states, value_states, outputs, output_grad, logsumexp, random_owner, random_slot,
):
    toks, heads, _ = queries.shape
    group = heads // n_head
    rows = toks * group
    span = toks * n_head
    blocks = span // BLK
    per_row = blocks * RND
    most = max(1, (per_row + n_seq - 1) // n_seq)
    pieces = 3 if toks % 3 == 0 else 1
    vmem = pl.BlockSpec(memory_space=pltpu.VMEM)
    smem = pl.BlockSpec(memory_space=pltpu.SMEM)
    hbm = pl.BlockSpec(memory_space=pl.ANY)
    dma = pltpu.SemaphoreType.DMA

    lse = jnp.transpose(logsumexp.reshape(toks, n_head, group), (1, 0, 2))
    lse = lse.reshape(n_head, rows // 128, 1, 128)
    kv = jnp.transpose(jnp.stack([key_states, value_states]), (2, 0, 1, 3))

    slots = n_seq * most
    step = BLK * group
    query_grad, kv_all = pl.pallas_call(
        functools.partial(fused, n_seq, n_head, most, blocks, pieces),
        out_shape=[
            jax.ShapeDtypeStruct((toks, heads, HD), BF16),
            jax.ShapeDtypeStruct((n_head, 2, toks, HD), BF16),
        ],
        in_specs=[smem, smem, hbm, hbm, hbm, vmem, vmem],
        out_specs=[hbm, vmem],
        scratch_shapes=[
            pltpu.SMEM((slots,), jnp.int32),
            pltpu.SMEM((per_row,), jnp.int32),
            pltpu.SMEM((slots,), jnp.int32),
            pltpu.VMEM((blocks, RND * BLK, step), BF16),
            pltpu.VMEM((n_head, toks, group, HD), BF16),
            pltpu.VMEM((n_head, toks, group, HD), BF16),
            pltpu.VMEM((n_head, rows // 128, 1, 128), F32),
            pltpu.VMEM((span, group, HD), BF16),
            pltpu.VMEM((span, group, HD), BF16),
            pltpu.VMEM((n_head * rows // 128, 1, 128), F32),
            pltpu.VMEM((n_head * rows // 128, 1, 128), F32),
            pltpu.VMEM((2, span + 2 * BLK, HD), BF16),
            pltpu.VMEM((2, G * BLK, HD), BF16),
            pltpu.VMEM((slots, BLK, HD), BF16),
            pltpu.VMEM((slots, BLK, HD), BF16),
            pltpu.VMEM((2, slots, BLK, HD), BF16),
            pltpu.VMEM((2, blocks, BLK, HD), BF16),
            pltpu.VMEM((2, span + 2 * BLK, HD), F32),
            pltpu.VMEM((2, G * BLK, HD), F32),
            pltpu.VMEM((blocks, HD, step), F32),
            pltpu.VMEM((span, group, HD), BF16),
            pltpu.VMEM((2, per_row, BLK, HD), BF16),
            pltpu.VMEM((2, slots, BLK, HD), BF16),
            pltpu.VMEM((2, 2, BLK, HD), BF16),
            pltpu.VMEM((2, 2, BLK, HD), BF16),
            pltpu.VMEM((2, G * BLK, HD), BF16),
            pltpu.VMEM((n_seq, 2, G * BLK, HD), BF16),
            pltpu.VMEM((2, span, HD), BF16),
            dma((6,)), dma((2, n_head)), dma((2, n_head)), dma((2, n_head)),
            dma((2, n_head)), dma((2, n_head)),
            dma((2, n_head, pieces)), dma((2, n_head, pieces)),
            dma((n_head,)), dma((n_head,)), dma((2, n_head)), dma((2, n_head)),
            dma((2, n_seq)), dma((2, n_seq)), dma((2, 2)), dma((2, 2)), dma((2,)), dma((2,)),
            dma((2, n_seq)), dma((2,)), dma((1,)), dma((n_seq,)),
            dma((2, n_seq)), dma((2, n_seq)),
        ],
        compiler_params=pltpu.CompilerParams(
            collective_id=0, has_side_effects=True, vmem_limit_bytes=60 << 20
        ),
        name="fused",
    )(random_owner.T, random_slot.T, queries, output_grad, outputs, kv, lse)

    key_grad = jnp.transpose(kv_all[:, 0], (1, 0, 2))
    value_grad = jnp.transpose(kv_all[:, 1], (1, 0, 2))
    return query_grad, key_grad, value_grad


def solution(mesh):
    wide = P(("seq", "head"), None, None)
    return jax.shard_map(
        functools.partial(per_device, mesh.shape["seq"], mesh.shape["head"]),
        mesh=mesh,
        in_specs=(wide, wide, wide, wide, wide, P(("seq", "head"), None), P(), P()),
        out_specs=(wide, wide, wide),
        check_vma=False,
    )
```

```python
import functools
import math

import jax
import jax.numpy as jnp
from jax import lax
from jax.experimental import pallas as pl
from jax.experimental.pallas import tpu as pltpu
from jax.sharding import PartitionSpec as P

HD = 128
BLK = 128
G = 2
RND = 3
MESH = pl.DeviceIdType.MESH
F32 = jnp.float32
BF16 = jnp.bfloat16
LOG2E = math.log2(math.e)


def greet(n_seq, n_head, seq, head):
    barrier = pltpu.get_barrier_semaphore()

    def to_head(d, c):
        pl.semaphore_signal(
            barrier, inc=1, device_id={"head": lax.rem(head + d, n_head)}, device_id_type=MESH
        )
        return c

    def to_seq(d, c):
        pl.semaphore_signal(
            barrier, inc=1, device_id={"seq": lax.rem(seq + d, n_seq)}, device_id_type=MESH
        )
        return c

    lax.fori_loop(1, n_head, to_head, 0)
    lax.fori_loop(1, n_seq, to_seq, 0)
    pl.semaphore_wait(barrier, n_head + n_seq - 2)


def remote(src, dst, send, recv, **where):
    return pltpu.make_async_remote_copy(
        src_ref=src,
        dst_ref=dst,
        send_sem=send,
        recv_sem=recv,
        device_id=where,
        device_id_type=MESH,
    )


def loop(low, high, body):
    def run(i, c):
        body(i)
        return c

    lax.fori_loop(low, high, run, 0)


def dot(a, b, ca, cb):
    return lax.dot_general(a, b, (((ca,), (cb,)), ((), ())), preferred_element_type=F32)


def pair_grads(k, v, shifts, q, g, delta, scaling):
    scores = dot(k, q, 1, 1) * (scaling * LOG2E)
    weights = jnp.concatenate(
        [jnp.exp2(scores[i * BLK : (i + 1) * BLK] - shift) for i, shift in enumerate(shifts)],
        axis=0,
    )
    score_grad = (weights * (dot(v, g, 1, 1) - delta)).astype(BF16)
    dv = dot(weights.astype(BF16), g, 1, 0)
    dk = dot(score_grad, q, 1, 0) * scaling
    return dk, dv, dot(k, score_grad, 0, 0)


def arrival_order(n_head, toks, blocks, pieces):
    size = toks // pieces
    stages = []
    for b in range(blocks):
        stage = -1
        for part in range(b * BLK // size, (b * BLK + BLK - 1) // size + 1):
            if part // pieces >= n_head // 2:
                stage = max(stage, part % pieces)
        stages.append((stage, b))
    return sorted(stages)


def tables(n_seq, most, blocks, seq, owner, slot, pick, pos, back):
    entries = [(b, j) for b in range(blocks) for j in range(RND)]
    mine = [owner[j, seq * blocks + b] for b, j in entries]
    for e, own in enumerate(mine):
        rank = jnp.int32(0)
        for other in mine[:e]:
            rank = rank + jnp.where(other == own, 1, 0)
        pos[e] = own * most + rank

    def scan(names, values, wanted, table, at, empty):
        count = jnp.int32(0)
        found = [jnp.int32(empty)] * most
        for name, value in zip(names, values):
            hit = name == wanted
            for m in range(most):
                found[m] = jnp.where(jnp.logical_and(hit, count == m), value, found[m])
            count = count + jnp.where(hit, 1, 0)
        for m in range(most):
            table[at * most + m] = found[m]

    def asked(p):
        names = [owner[j, p * blocks + b] for b, j in entries]
        values = [slot[j, p * blocks + b] for b, j in entries]
        scan(names, values, seq, pick, p, -1)

    def answered(p):
        names = [owner[j, seq * blocks + b] for b, j in entries]
        scan(names, [jnp.int32(e) for e in range(len(entries))], p, back, p, 0)

    loop(0, n_seq, asked)
    loop(0, n_seq, answered)


def fused(
    n_seq, n_head, most, blocks, pieces,
    owner, slot, q_in, g_in, o_in, k_raw, v_raw, lse_in,
    dq_out, dk_out, dv_out,
    kv_in, kv_out, lse_own, pick, pos, back,
    far_weights, g_own, o_own, delta_own,
    q_all, g_all, lse_all, delta_all, kv_ext, glob, rand_k, rand_v, picked, held, acc, gacc, dq_acc, dq_all,
    rpart, rback, halo_part, halo, gpart, gall, kv_sum,
    ls, os, ks, kr, ts, tr, qs, qr, ds, dr, es, er,
    ss, sr, ns, nr, hs, hr, gs, gr, ps, pr, rs, rr,
):
    seq, head = lax.axis_index("seq"), lax.axis_index("head")
    toks = kv_in.shape[2]
    group = q_in.shape[1] // n_head
    rows = toks * group
    span = n_head * toks
    lines = rows // 128
    step = BLK * group
    half = n_head // 2
    size = toks // pieces
    scaling = 1.0 / HD**0.5
    turn = head // half
    far_half = range(half, n_head)
    rand = (rand_k, rand_v)
    plan = arrival_order(n_head, toks, blocks, pieces)

    def partner(d):
        base = lax.rem(head + 2 * (d // 2), n_head)
        return base + (1 - 2 * lax.rem(base, 2)) if d % 2 else base

    sends = list(range(2, n_head)) + [1]
    here = pl.ds(pl.multiple_of(head * toks, toks), toks)
    kv_rows = pl.ds(pl.multiple_of(BLK + head * toks, 32), toks)
    line_rows = pl.ds(head * lines, lines)

    def heads_of(ref, peer):
        return ref.at[:, pl.ds(pl.multiple_of(peer * group, group), group), :]

    own = [
        pltpu.make_async_copy(kv_in.at[head, 0], kv_ext.at[0, kv_rows, :], ls.at[0]),
        pltpu.make_async_copy(kv_in.at[head, 1], kv_ext.at[1, kv_rows, :], ls.at[1]),
        None,
        pltpu.make_async_copy(heads_of(q_in, head), q_all.at[here], ls.at[3]),
        pltpu.make_async_copy(heads_of(g_in, head), g_all.at[here], ls.at[4]),
    ]
    taken = [
        pltpu.make_async_copy(heads_of(src, p), dst.at[p], os.at[i, p])
        for p in range(n_head)
        for i, (src, dst) in enumerate(((g_in, g_own), (o_in, o_own)))
    ]
    for copy in taken + own[3:]:
        copy.start()

    def spread(part):
        whole = (k_raw, v_raw)[part][...].astype(F32).reshape(toks, n_head * HD).astype(BF16)
        for p in range(n_head):
            kv_in[p, part] = whole[:, p * HD : (p + 1) * HD]

    spread(0)
    spread(1)
    for copy in own[:2]:
        copy.start()
    greet(n_seq, n_head, seq, head)

    def kv_head(part, d):
        peer = partner(d)
        return remote(
            kv_in.at[peer, part], kv_ext.at[part, kv_rows, :], ks.at[part, d], kr.at[part, d], head=peer
        )

    def line_head(kind, d):
        peer = partner(d)
        src, dst = ((lse_own, lse_all), (delta_own, delta_all))[kind]
        return remote(src.at[peer], dst.at[line_rows], ts.at[kind, d], tr.at[kind, d], head=peer)

    def mirrored(side, i, n):
        return i + side * (n - 1 - 2 * i)

    def piece_send(kind, d, i):
        peer = partner(d)
        side = peer // half
        off = mirrored(side, i, pieces) * size
        src = (q_in, g_in)[kind].at[
            pl.ds(off, size), pl.ds(pl.multiple_of(peer * group, group), group), :
        ]
        dst = (q_all, g_all)[kind].at[pl.ds(head * toks + off, size)]
        return remote(
            src, dst, qs.at[kind, d, i], qr.at[kind, mirrored(side, head, n_head), i], head=peer
        )

    def piece_wait(kind, v, i):
        off = mirrored(turn, v, n_head) * toks + mirrored(turn, i, pieces) * size
        dst = (q_all, g_all)[kind].at[pl.ds(off, size)]
        remote(dst, dst, qs.at[kind, 0, i], qr.at[kind, v, i], head=partner(1)).wait_recv()

    for part in range(2):
        for d in sends:
            kv_head(part, d).start()
    for kind in range(2):
        for i in range(pieces):
            piece_send(kind, 1, i).start()
    for kind in range(2):
        for d in range(2, n_head):
            piece_send(kind, d, 0).start()

    tables(n_seq, most, blocks, seq, owner, slot, pick, pos, back)

    up, down = lax.rem(seq + 1, n_seq), lax.rem(seq + n_seq - 1, n_seq)

    def to_up(part):
        return remote(
            kv_ext.at[part, pl.ds(span, BLK), :], kv_ext.at[part, pl.ds(0, BLK), :],
            ns.at[part, 0], nr.at[part, 0], seq=up,
        )

    def to_down(part):
        return remote(
            kv_ext.at[part, pl.ds(BLK, BLK), :], kv_ext.at[part, pl.ds(BLK + span, BLK), :],
            ns.at[part, 1], nr.at[part, 1], seq=down,
        )

    def slots_of(peer):
        return pl.ds(peer * most, most)

    def rand_copy(part, d):
        peer = lax.rem(seq + d, n_seq)
        return remote(
            picked.at[part, slots_of(peer)], rand[part].at[slots_of(seq)],
            ss.at[part, d], sr.at[part, d], seq=peer,
        )

    def glob_copy(part, d):
        return remote(
            kv_ext.at[part, pl.ds(BLK, G * BLK), :], glob.at[part], gs.at[part, d], gr.at[part], seq=d
        )

    for part in range(2):
        own[part].wait()
        for d in range(1, n_head):
            kv_head(part, d).wait_recv()
        for block in range(blocks):
            held[part, block] = kv_ext[part, (block + 1) * BLK : (block + 2) * BLK, :]
        def fill(i):
            picked[part, i] = held[part, jnp.maximum(pick[i], 0)]

        loop(0, n_seq * most, fill)
        to_up(part).start()
        to_down(part).start()

        @pl.when(seq == 0)
        def _():
            loop(1, n_seq, lambda d: glob_copy(part, d).start())
            glob[part] = kv_ext[part, BLK : BLK + G * BLK, :]

        loop(1, n_seq, lambda d: rand_copy(part, d).start())
        rand[part][slots_of(seq)] = picked[part, slots_of(seq)]

    for copy in taken:
        copy.wait()
    ones = jnp.ones((HD, 128), BF16)
    eye = (
        lax.broadcasted_iota(jnp.int32, (128, 128), 0)
        == lax.broadcasted_iota(jnp.int32, (128, 128), 1)
    ).astype(F32)
    cut = 32
    flat = cut * group
    for p in range(n_head):
        def row_delta(c):
            at = pl.ds(pl.multiple_of(c * cut, cut), cut)
            full = g_own[p, at].reshape(flat, HD).astype(F32) * o_own[p, at].reshape(flat, HD).astype(F32)
            high = full.astype(BF16)
            low = (full - high.astype(F32)).astype(BF16)
            sums = dot(high, ones, 1, 0) + dot(low, ones, 1, 0)
            for r in range(flat // 128):
                line = jnp.sum(sums[r * 128 : (r + 1) * 128] * eye, axis=0, keepdims=True)
                delta_own[p, c * (flat // 128) + r] = line

        loop(0, toks // cut, row_delta)
    per_line = 128 // group
    lane = lax.broadcasted_iota(jnp.int32, (per_line, 128), 1)
    term = (lane // group == lax.broadcasted_iota(jnp.int32, (per_line, 128), 0)).astype(BF16)
    terms = jnp.concatenate([term] * 3, axis=0)
    wide = lax.broadcasted_iota(jnp.int32, (n_head * group, 128), 0)
    keep = wide % group == lax.broadcasted_iota(jnp.int32, (n_head * group, 128), 1) % group
    for r in range(toks // per_line):
        full = lse_in[:, r * per_line : (r + 1) * per_line]
        high = full.astype(BF16)
        rest = full - high.astype(F32)
        middle = rest.astype(BF16)
        low = (rest - middle.astype(F32)).astype(BF16)
        sums = dot(jnp.concatenate([high, middle, low], axis=1), terms, 1, 0)
        sums = jnp.where(keep, sums, 0.0)
        for p in range(n_head):
            lse_own[p, r] = jnp.sum(sums[p * group : (p + 1) * group], axis=0, keepdims=True)
    lse_all[line_rows] = lse_own[head]
    delta_all[line_rows] = delta_own[head]
    for d in sends:
        for kind in range(2):
            line_head(kind, d).start()
    for i in range(1, pieces):
        for kind in range(2):
            for d in range(2, n_head):
                piece_send(kind, d, i).start()

    acc[...] = jnp.zeros_like(acc)
    gacc[...] = jnp.zeros_like(gacc)
    for part in range(2):
        to_up(part).wait()
        to_down(part).wait()

    @pl.when(seq > 0)
    def _():
        for part in range(2):
            glob_copy(part, 0).wait_recv()

    for copy in own[3:]:
        copy.wait()
    soon = [1] if half == 2 else list(range(1, n_head))
    for d in soon:
        for kind in range(2):
            line_head(kind, d).wait_recv()
    for kind in range(2):
        for k in range(1, half):
            v = lax.rem(mirrored(turn, head, n_head) + k, half)
            for i in range(pieces):
                piece_wait(kind, v, i)

    def landed(i):
        if i == 0:
            for d in range(1, n_head):
                if d not in soon:
                    line_head(0, d).wait_recv()
                    line_head(1, d).wait_recv()
        for kind in range(2):
            for v in far_half:
                piece_wait(kind, v, i)

    def block_at(i):
        b = jnp.int32(plan[0][1])
        for k in range(1, blocks):
            b = jnp.where(i == k, plan[k][1], b)
        return mirrored(turn, b, blocks)

    def operands(b):
        spot = pl.ds(pl.multiple_of(b * BLK, BLK), BLK)
        per = step // 128

        def lanes(ref):
            tile = ref[pl.ds(b * per, per)]
            return jnp.concatenate([tile[r] for r in range(per)], axis=1)

        flat = (step, HD)
        return q_all[spot].reshape(flat), g_all[spot].reshape(flat), lanes(lse_all) * LOG2E, lanes(delta_all)

    def hidden(okay):
        return jnp.where(okay, 0.0, 1e30).astype(F32)

    def near(i):
        b = block_at(i)
        q, g, lse, delta = operands(b)
        at = pl.multiple_of(b * BLK, BLK)
        win = pl.ds(at, 3 * BLK)
        dk, dv, dq = pair_grads(glob[0], glob[1], [lse] * G, q, g, delta, scaling)
        gacc[0] += dk
        gacc[1] += dv
        block = seq * blocks + b
        shifts = []
        for j in range(-1, 2):
            okay = jnp.logical_and(block + j >= G, block + j <= n_seq * blocks - 1)
            shifts.append(lse + hidden(okay))
        dk, dv, more = pair_grads(kv_ext[0, win, :], kv_ext[1, win, :], shifts, q, g, delta, scaling)
        acc[0, win, :] += dk
        acc[1, win, :] += dv
        dq_acc[b] = dq + more

    def found(part, b):
        return jnp.concatenate([rand[part][pos[b * RND + j]] for j in range(RND)], axis=0)

    def far_values(i):
        b = block_at(i)
        q, g, lse, _ = operands(b)
        block = seq * blocks + b
        scores = dot(found(0, b), q, 1, 1) * (scaling * LOG2E)
        parts = []
        for j in range(RND):
            other = owner[j, block] * blocks + slot[j, block]
            okay = jnp.logical_and(other >= G, jnp.abs(other - block) >= 2)
            shift = lse + hidden(okay)
            parts.append(jnp.exp2(scores[j * BLK : (j + 1) * BLK] - shift).astype(BF16))
        weights = jnp.concatenate(parts, axis=0)
        far_weights[b] = weights
        dv = dot(weights, g, 1, 0)
        for j in range(RND):
            rpart[1, b * RND + j] = dv[j * BLK : (j + 1) * BLK].astype(BF16)

    def far_keys(i):
        b = block_at(i)
        q, g, _, delta = operands(b)
        at = pl.multiple_of(b * BLK, BLK)
        rise = dot(found(1, b), g, 1, 1) - delta
        score_grad = (far_weights[b].astype(F32) * rise).astype(BF16)
        dk = dot(score_grad, q, 1, 0) * scaling
        for j in range(RND):
            rpart[0, b * RND + j] = dk[j * BLK : (j + 1) * BLK].astype(BF16)
        total = dq_acc[b] + dot(found(0, b), score_grad, 0, 0)
        dq_all[pl.ds(at, BLK)] = (total.T * scaling).astype(BF16).reshape(BLK, group, HD)

    last = pieces - 1
    early = sum(stage < last for stage, _ in plan)
    firsts = {}
    for i, (stage, _) in enumerate(plan):
        for s in range(stage + 1):
            firsts.setdefault(s, i)

    def near_early(i):
        for s in range(last):
            if s in firsts and firsts[s] < early:
                @pl.when(i == firsts[s])
                def _():
                    landed(s)

        near(i)

    loop(0, early, near_early)
    for s in range(last):
        if s not in firsts or firsts[s] >= early:
            landed(s)
    loop(1, n_seq, lambda d: rand_copy(0, d).wait())
    loop(0, early, far_values)
    landed(last)
    loop(early, blocks, far_values)
    loop(1, n_seq, lambda d: rand_copy(1, d).wait_send())

    def back_copy(part, d):
        peer = lax.rem(seq + d, n_seq)
        return remote(
            picked.at[part, slots_of(peer)], rback.at[part, slots_of(seq)],
            rs.at[part, d], rr.at[part, d], seq=peer,
        )

    def gather(part):
        def move(i):
            picked[part, i] = rpart[part, back[i]]

        loop(0, n_seq * most, move)

    gather(1)
    loop(1, n_seq, lambda d: back_copy(1, d).start())
    loop(early, blocks, near)

    halo_part[0] = acc[:, 0:BLK, :].astype(BF16)
    halo_part[1] = acc[:, BLK + span :, :].astype(BF16)
    gpart[...] = gacc[...].astype(BF16)

    def dq_copy(d):
        peer = partner(d)
        src = dq_all.at[pl.ds(pl.multiple_of(peer * toks, toks), toks)]
        return remote(src, heads_of(dq_out, head), ds.at[d], dr.at[d], head=peer)

    def kv_copy(part, d):
        peer = partner(d)
        src = kv_sum.at[part, pl.ds(pl.multiple_of(peer * toks, 32), toks), :]
        return remote(src, kv_out.at[head, part], es.at[part, d], er.at[part, d], head=peer)

    def part_copy():
        return remote(gpart, gall.at[seq], ps.at[0], pr.at[seq], seq=0)

    down_grad = remote(halo_part.at[0], halo.at[0], hs.at[0], hr.at[0], seq=down)
    up_grad = remote(halo_part.at[1], halo.at[1], hs.at[1], hr.at[1], seq=up)
    down_grad.start()
    up_grad.start()

    @pl.when(seq > 0)
    def _():
        part_copy().start()

    loop(1, n_seq, lambda d: rand_copy(1, d).wait_recv())
    loop(0, blocks, far_keys)
    gather(0)
    loop(1, n_seq, lambda d: back_copy(0, d).start())
    own_dq = pltpu.make_async_copy(dq_all.at[here], heads_of(dq_out, head), ls.at[5])
    for d in sends:
        dq_copy(d).start()
    own_dq.start()
    for part in range(2):
        rback[part, slots_of(seq)] = picked[part, slots_of(seq)]

    for d in range(1, n_head):
        for kind in range(2):
            kv_head(kind, d).wait_send()
            line_head(kind, d).wait_send()
            for i in range(pieces):
                piece_send(kind, d, i).wait_send()

    def absorb(part, d):
        base = lax.rem(seq + n_seq - d, n_seq) * most

        def block_sum(block):
            over = pl.ds(pl.multiple_of(block * BLK + BLK, BLK), BLK)
            value = acc[part, over, :]
            for m in range(most):
                share = jnp.where(pick[base + m] == block, 1.0, 0.0).astype(F32)
                value = value + share * rback[part, base + m].astype(F32)
            acc[part, over, :] = value

        loop(0, blocks, block_sum)

    absorb(1, 0)
    absorb(0, 0)

    @pl.when(seq == 0)
    def _():
        for part in range(2):
            loop(1, n_seq, lambda d: glob_copy(part, d).wait_send())
        gall[0] = gpart[...]

    def finish(part):
        for d in range(1, n_head):
            kv_copy(part, d).wait()
        whole = jnp.concatenate([kv_out[p, part] for p in range(n_head)], axis=1).astype(F32)
        (dk_out, dv_out)[part][...] = whole.reshape(toks, n_head, HD).astype(BF16)

    for part in (1, 0):
        def take(d):
            back_copy(part, d).wait()
            absorb(part, d)

        loop(1, n_seq, take)
        if part:
            @pl.when(seq == 0)
            def _():
                def arrive(d):
                    remote(gpart, gall.at[d], ps.at[0], pr.at[d], seq=0).wait_recv()

                loop(1, n_seq, arrive)

                def add(d):
                    gacc[...] += gall[d].astype(F32)

                loop(1, n_seq, add)
                acc[:, BLK : BLK + G * BLK, :] += gacc[...]

            @pl.when(seq > 0)
            def _():
                part_copy().wait_send()

            down_grad.wait()
            up_grad.wait()
            acc[:, BLK : 2 * BLK, :] += halo[1].astype(F32)
            acc[:, span : span + BLK, :] += halo[0].astype(F32)
        kv_sum[part] = acc[part, BLK : BLK + span, :].astype(BF16)
        for d in sends:
            kv_copy(part, d).start()
        kv_out[head, part] = kv_sum[part, pl.ds(pl.multiple_of(head * toks, 32), toks), :]
        if part == 0:
            own_dq.wait()
            for d in range(1, n_head):
                dq_copy(d).wait()
            finish(1)
            finish(0)


def per_device(
    n_seq, n_head,
    queries, key_states, value_states, outputs, output_grad, logsumexp, random_owner, random_slot,
):
    toks, heads, _ = queries.shape
    group = heads // n_head
    rows = toks * group
    span = toks * n_head
    blocks = span // BLK
    per_row = blocks * RND
    most = max(1, (per_row + n_seq - 1) // n_seq)
    pieces = 3 if toks % 3 == 0 else 1
    vmem = pl.BlockSpec(memory_space=pltpu.VMEM)
    smem = pl.BlockSpec(memory_space=pltpu.SMEM)
    hbm = pl.BlockSpec(memory_space=pl.ANY)
    dma = pltpu.SemaphoreType.DMA

    slots = n_seq * most
    step = BLK * group
    return pl.pallas_call(
        functools.partial(fused, n_seq, n_head, most, blocks, pieces),
        out_shape=[
            jax.ShapeDtypeStruct((toks, heads, HD), BF16),
            jax.ShapeDtypeStruct((toks, n_head, HD), BF16),
            jax.ShapeDtypeStruct((toks, n_head, HD), BF16),
        ],
        in_specs=[smem, smem, hbm, hbm, hbm, vmem, vmem, vmem],
        out_specs=[hbm, vmem, vmem],
        scratch_shapes=[
            pltpu.VMEM((n_head, 2, toks, HD), BF16),
            pltpu.VMEM((n_head, 2, toks, HD), BF16),
            pltpu.VMEM((n_head, rows // 128, 1, 128), F32),
            pltpu.SMEM((slots,), jnp.int32),
            pltpu.SMEM((per_row,), jnp.int32),
            pltpu.SMEM((slots,), jnp.int32),
            pltpu.VMEM((blocks, RND * BLK, step), BF16),
            pltpu.VMEM((n_head, toks, group, HD), BF16),
            pltpu.VMEM((n_head, toks, group, HD), BF16),
            pltpu.VMEM((n_head, rows // 128, 1, 128), F32),
            pltpu.VMEM((span, group, HD), BF16),
            pltpu.VMEM((span, group, HD), BF16),
            pltpu.VMEM((n_head * rows // 128, 1, 128), F32),
            pltpu.VMEM((n_head * rows // 128, 1, 128), F32),
            pltpu.VMEM((2, span + 2 * BLK, HD), BF16),
            pltpu.VMEM((2, G * BLK, HD), BF16),
            pltpu.VMEM((slots, BLK, HD), BF16),
            pltpu.VMEM((slots, BLK, HD), BF16),
            pltpu.VMEM((2, slots, BLK, HD), BF16),
            pltpu.VMEM((2, blocks, BLK, HD), BF16),
            pltpu.VMEM((2, span + 2 * BLK, HD), F32),
            pltpu.VMEM((2, G * BLK, HD), F32),
            pltpu.VMEM((blocks, HD, step), F32),
            pltpu.VMEM((span, group, HD), BF16),
            pltpu.VMEM((2, per_row, BLK, HD), BF16),
            pltpu.VMEM((2, slots, BLK, HD), BF16),
            pltpu.VMEM((2, 2, BLK, HD), BF16),
            pltpu.VMEM((2, 2, BLK, HD), BF16),
            pltpu.VMEM((2, G * BLK, HD), BF16),
            pltpu.VMEM((n_seq, 2, G * BLK, HD), BF16),
            pltpu.VMEM((2, span, HD), BF16),
            dma((6,)), dma((2, n_head)), dma((2, n_head)), dma((2, n_head)),
            dma((2, n_head)), dma((2, n_head)),
            dma((2, n_head, pieces)), dma((2, n_head, pieces)),
            dma((n_head,)), dma((n_head,)), dma((2, n_head)), dma((2, n_head)),
            dma((2, n_seq)), dma((2, n_seq)), dma((2, 2)), dma((2, 2)), dma((2,)), dma((2,)),
            dma((2, n_seq)), dma((2,)), dma((1,)), dma((n_seq,)),
            dma((2, n_seq)), dma((2, n_seq)),
        ],
        compiler_params=pltpu.CompilerParams(
            collective_id=0, has_side_effects=True, vmem_limit_bytes=60 << 20
        ),
        name="fused",
    )(
        random_owner.T, random_slot.T, queries, output_grad, outputs,
        key_states, value_states, logsumexp.T,
    )


def solution(mesh):
    wide = P(("seq", "head"), None, None)
    return jax.shard_map(
        functools.partial(per_device, mesh.shape["seq"], mesh.shape["head"]),
        mesh=mesh,
        in_specs=(wide, wide, wide, wide, wide, P(("seq", "head"), None), P(), P()),
        out_specs=(wide, wide, wide),
        check_vma=False,
    )
```

```python
import functools
import math

import jax
import jax.numpy as jnp
from jax import lax
from jax.experimental import pallas as pl
from jax.experimental.pallas import tpu as pltpu
from jax.sharding import PartitionSpec as P

HD = 128
BLK = 128
G = 2
RND = 3
MESH = pl.DeviceIdType.MESH
F32 = jnp.float32
BF16 = jnp.bfloat16
LOG2E = math.log2(math.e)
LIFT = 8.0


def greet(n_seq, n_head, seq, head):
    barrier = pltpu.get_barrier_semaphore()

    def to_head(d, c):
        pl.semaphore_signal(
            barrier, inc=1, device_id={"head": lax.rem(head + d, n_head)}, device_id_type=MESH
        )
        return c

    def to_seq(d, c):
        pl.semaphore_signal(
            barrier, inc=1, device_id={"seq": lax.rem(seq + d, n_seq)}, device_id_type=MESH
        )
        return c

    lax.fori_loop(1, n_head, to_head, 0)
    lax.fori_loop(1, n_seq, to_seq, 0)
    pl.semaphore_wait(barrier, n_head + n_seq - 2)


def remote(src, dst, send, recv, **where):
    return pltpu.make_async_remote_copy(
        src_ref=src,
        dst_ref=dst,
        send_sem=send,
        recv_sem=recv,
        device_id=where,
        device_id_type=MESH,
    )


def loop(low, high, body):
    def run(i, c):
        body(i)
        return c

    lax.fori_loop(low, high, run, 0)


def dot(a, b, ca, cb):
    return lax.dot_general(a, b, (((ca,), (cb,)), ((), ())), preferred_element_type=F32)


def pair_grads(k, v, shifts, q, g, delta, scaling):
    scores = dot(k, q, 1, 1) * (scaling * LOG2E)
    weights = jnp.concatenate(
        [jnp.exp2(scores[i * BLK : (i + 1) * BLK] - shift) for i, shift in enumerate(shifts)],
        axis=0,
    )
    score_grad = (weights * (dot(v, g, 1, 1) - delta)).astype(BF16)
    dv = dot(weights.astype(BF16), g, 1, 0)
    dk = dot(score_grad, q, 1, 0) * scaling
    return dk, dv, dot(k, score_grad, 0, 0)


def arrival_order(n_head, toks, blocks, pieces):
    size = toks // pieces
    stages = []
    for b in range(blocks):
        stage = -1
        for part in range(b * BLK // size, (b * BLK + BLK - 1) // size + 1):
            if part // pieces >= n_head // 2:
                stage = max(stage, part % pieces)
        stages.append((stage, b))
    return sorted(stages)


def tables(n_seq, most, blocks, seq, owner, slot, pick, pos, back):
    entries = [(b, j) for b in range(blocks) for j in range(RND)]
    mine = [owner[j, seq * blocks + b] for b, j in entries]
    for e, own in enumerate(mine):
        rank = jnp.int32(0)
        for other in mine[:e]:
            rank = rank + jnp.where(other == own, 1, 0)
        pos[e] = own * most + rank

    def scan(names, values, wanted, table, at, empty):
        count = jnp.int32(0)
        found = [jnp.int32(empty)] * most
        for name, value in zip(names, values):
            hit = name == wanted
            for m in range(most):
                found[m] = jnp.where(jnp.logical_and(hit, count == m), value, found[m])
            count = count + jnp.where(hit, 1, 0)
        for m in range(most):
            table[at * most + m] = found[m]

    def asked(p):
        names = [owner[j, p * blocks + b] for b, j in entries]
        values = [slot[j, p * blocks + b] for b, j in entries]
        scan(names, values, seq, pick, p, -1)

    def answered(p):
        names = [owner[j, seq * blocks + b] for b, j in entries]
        scan(names, [jnp.int32(e) for e in range(len(entries))], p, back, p, 0)

    loop(0, n_seq, asked)
    loop(0, n_seq, answered)


def fused(
    n_seq, n_head, most, blocks, pieces,
    owner, slot, q_in, g_in, o_in, k_raw, v_raw, lse_in,
    dq_out, dk_out, dv_out,
    kv_in, kv_out, lse_own, pick, pos, back,
    far_weights, g_own, o_own, delta_own,
    q_all, g_all, lse_all, delta_all, kv_ext, glob, rand_k, rand_v, picked, held, acc, gacc, dq_acc, dq_all,
    rpart, rback, halo_part, halo, gpart, gall, kv_sum,
    ls, os, ks, kr, ts, tr, qs, qr, ds, dr, es, er,
    ss, sr, ns, nr, hs, hr, gs, gr, ps, pr, rs, rr,
):
    seq, head = lax.axis_index("seq"), lax.axis_index("head")
    toks = kv_in.shape[2]
    group = q_in.shape[1] // n_head
    rows = toks * group
    span = n_head * toks
    lines = rows // 128
    step = BLK * group
    half = n_head // 2
    size = toks // pieces
    scaling = 1.0 / HD**0.5
    turn = head // half
    far_half = range(half, n_head)
    rand = (rand_k, rand_v)
    plan = arrival_order(n_head, toks, blocks, pieces)

    def partner(d):
        base = lax.rem(head + 2 * (d // 2), n_head)
        return base + (1 - 2 * lax.rem(base, 2)) if d % 2 else base

    sends = list(range(2, n_head)) + [1]
    here = pl.ds(pl.multiple_of(head * toks, toks), toks)
    kv_rows = pl.ds(pl.multiple_of(BLK + head * toks, 32), toks)
    line_rows = pl.ds(head * lines, lines)

    def heads_of(ref, peer):
        return ref.at[:, pl.ds(pl.multiple_of(peer * group, group), group), :]

    own = [
        pltpu.make_async_copy(kv_in.at[head, 0], kv_ext.at[0, kv_rows, :], ls.at[0]),
        pltpu.make_async_copy(kv_in.at[head, 1], kv_ext.at[1, kv_rows, :], ls.at[1]),
        None,
        pltpu.make_async_copy(heads_of(q_in, head), q_all.at[here], ls.at[3]),
        pltpu.make_async_copy(heads_of(g_in, head), g_all.at[here], ls.at[4]),
    ]
    taken = [
        pltpu.make_async_copy(heads_of(src, p), dst.at[p], os.at[i, p])
        for p in range(n_head)
        for i, (src, dst) in enumerate(((g_in, g_own), (o_in, o_own)))
    ]
    for copy in taken + own[3:]:
        copy.start()

    def spread(part):
        whole = (k_raw, v_raw)[part][...].astype(F32).reshape(toks, n_head * HD).astype(BF16)
        for p in range(n_head):
            kv_in[p, part] = whole[:, p * HD : (p + 1) * HD]

    spread(0)
    spread(1)
    for copy in own[:2]:
        copy.start()
    greet(n_seq, n_head, seq, head)

    def kv_head(part, d):
        peer = partner(d)
        return remote(
            kv_in.at[peer, part], kv_ext.at[part, kv_rows, :], ks.at[part, d], kr.at[part, d], head=peer
        )

    def line_head(kind, d):
        peer = partner(d)
        src, dst = ((lse_own, lse_all), (delta_own, delta_all))[kind]
        return remote(src.at[peer], dst.at[line_rows], ts.at[kind, d], tr.at[kind, d], head=peer)

    def mirrored(side, i, n):
        return i + side * (n - 1 - 2 * i)

    def piece_send(kind, d, i):
        peer = partner(d)
        side = peer // half
        off = mirrored(side, i, pieces) * size
        src = (q_in, g_in)[kind].at[
            pl.ds(off, size), pl.ds(pl.multiple_of(peer * group, group), group), :
        ]
        dst = (q_all, g_all)[kind].at[pl.ds(head * toks + off, size)]
        return remote(
            src, dst, qs.at[kind, d, i], qr.at[kind, mirrored(side, head, n_head), i], head=peer
        )

    def piece_wait(kind, v, i):
        off = mirrored(turn, v, n_head) * toks + mirrored(turn, i, pieces) * size
        dst = (q_all, g_all)[kind].at[pl.ds(off, size)]
        remote(dst, dst, qs.at[kind, 0, i], qr.at[kind, v, i], head=partner(1)).wait_recv()

    for part in range(2):
        for d in sends:
            kv_head(part, d).start()
    for kind in range(2):
        for i in range(pieces):
            piece_send(kind, 1, i).start()
    for kind in range(2):
        for d in range(2, n_head):
            piece_send(kind, d, 0).start()

    tables(n_seq, most, blocks, seq, owner, slot, pick, pos, back)

    up, down = lax.rem(seq + 1, n_seq), lax.rem(seq + n_seq - 1, n_seq)

    def to_up(part):
        return remote(
            kv_ext.at[part, pl.ds(span, BLK), :], kv_ext.at[part, pl.ds(0, BLK), :],
            ns.at[part, 0], nr.at[part, 0], seq=up,
        )

    def to_down(part):
        return remote(
            kv_ext.at[part, pl.ds(BLK, BLK), :], kv_ext.at[part, pl.ds(BLK + span, BLK), :],
            ns.at[part, 1], nr.at[part, 1], seq=down,
        )

    def slots_of(peer):
        return pl.ds(peer * most, most)

    def rand_copy(part, d):
        peer = lax.rem(seq + d, n_seq)
        return remote(
            picked.at[part, slots_of(peer)], rand[part].at[slots_of(seq)],
            ss.at[part, d], sr.at[part, d], seq=peer,
        )

    def glob_copy(part, d):
        return remote(
            kv_ext.at[part, pl.ds(BLK, G * BLK), :], glob.at[part], gs.at[part, d], gr.at[part], seq=d
        )

    for part in range(2):
        own[part].wait()
        for d in range(1, n_head):
            kv_head(part, d).wait_recv()
        for block in range(blocks):
            held[part, block] = kv_ext[part, (block + 1) * BLK : (block + 2) * BLK, :]
        def fill(i):
            picked[part, i] = held[part, jnp.maximum(pick[i], 0)]

        loop(0, n_seq * most, fill)
        to_up(part).start()
        to_down(part).start()

        @pl.when(seq == 0)
        def _():
            loop(1, n_seq, lambda d: glob_copy(part, d).start())
            glob[part] = kv_ext[part, BLK : BLK + G * BLK, :]

        loop(1, n_seq, lambda d: rand_copy(part, d).start())
        rand[part][slots_of(seq)] = picked[part, slots_of(seq)]

    for copy in taken:
        copy.wait()
    ones = jnp.ones((HD, 128), BF16)
    eye = (
        lax.broadcasted_iota(jnp.int32, (128, 128), 0)
        == lax.broadcasted_iota(jnp.int32, (128, 128), 1)
    ).astype(F32)
    cut = 32
    flat = cut * group
    for p in range(n_head):
        def row_delta(c):
            at = pl.ds(pl.multiple_of(c * cut, cut), cut)
            full = g_own[p, at].reshape(flat, HD).astype(F32) * o_own[p, at].reshape(flat, HD).astype(F32)
            high = full.astype(BF16)
            low = (full - high.astype(F32)).astype(BF16)
            sums = dot(high, ones, 1, 0) + dot(low, ones, 1, 0)
            for r in range(flat // 128):
                line = jnp.sum(sums[r * 128 : (r + 1) * 128] * eye, axis=0, keepdims=True)
                delta_own[p, c * (flat // 128) + r] = line

        loop(0, toks // cut, row_delta)
    per_line = 128 // group
    lane = lax.broadcasted_iota(jnp.int32, (per_line, 128), 1)
    term = (lane // group == lax.broadcasted_iota(jnp.int32, (per_line, 128), 0)).astype(BF16)
    terms = jnp.concatenate([term] * 3, axis=0)
    wide = lax.broadcasted_iota(jnp.int32, (n_head * group, 128), 0)
    keep = wide % group == lax.broadcasted_iota(jnp.int32, (n_head * group, 128), 1) % group
    for r in range(toks // per_line):
        full = lse_in[:, r * per_line : (r + 1) * per_line]
        high = full.astype(BF16)
        rest = full - high.astype(F32)
        middle = rest.astype(BF16)
        low = (rest - middle.astype(F32)).astype(BF16)
        sums = dot(jnp.concatenate([high, middle, low], axis=1), terms, 1, 0)
        sums = jnp.where(keep, sums, 0.0)
        for p in range(n_head):
            lse_own[p, r] = jnp.sum(sums[p * group : (p + 1) * group], axis=0, keepdims=True)
    lse_all[line_rows] = lse_own[head]
    delta_all[line_rows] = delta_own[head]
    for d in sends:
        for kind in range(2):
            line_head(kind, d).start()
    for i in range(1, pieces):
        for kind in range(2):
            for d in range(2, n_head):
                piece_send(kind, d, i).start()

    acc[...] = jnp.zeros_like(acc)
    gacc[...] = jnp.zeros_like(gacc)
    for part in range(2):
        to_up(part).wait()
        to_down(part).wait()

    @pl.when(seq > 0)
    def _():
        for part in range(2):
            glob_copy(part, 0).wait_recv()

    for copy in own[3:]:
        copy.wait()
    soon = [1] if half == 2 else list(range(1, n_head))
    for d in soon:
        for kind in range(2):
            line_head(kind, d).wait_recv()
    for kind in range(2):
        for k in range(1, half):
            v = lax.rem(mirrored(turn, head, n_head) + k, half)
            for i in range(pieces):
                piece_wait(kind, v, i)

    def landed(i):
        if i == 0:
            for d in range(1, n_head):
                if d not in soon:
                    line_head(0, d).wait_recv()
                    line_head(1, d).wait_recv()
        for kind in range(2):
            for v in far_half:
                piece_wait(kind, v, i)

    def block_at(i):
        b = jnp.int32(plan[0][1])
        for k in range(1, blocks):
            b = jnp.where(i == k, plan[k][1], b)
        return mirrored(turn, b, blocks)

    def operands(b):
        spot = pl.ds(pl.multiple_of(b * BLK, BLK), BLK)
        per = step // 128

        def lanes(ref):
            tile = ref[pl.ds(b * per, per)]
            return jnp.concatenate([tile[r] for r in range(per)], axis=1)

        flat = (step, HD)
        return q_all[spot].reshape(flat), g_all[spot].reshape(flat), lanes(lse_all) * LOG2E, lanes(delta_all)

    def hidden(okay):
        return jnp.where(okay, 0.0, 1e30).astype(F32)

    def near(i):
        b = block_at(i)
        q, g, lse, delta = operands(b)
        at = pl.multiple_of(b * BLK, BLK)
        win = pl.ds(at, 3 * BLK)
        dk, dv, dq = pair_grads(glob[0], glob[1], [lse] * G, q, g, delta, scaling)
        gacc[0] += dk
        gacc[1] += dv
        block = seq * blocks + b
        shifts = []
        for j in range(-1, 2):
            okay = jnp.logical_and(block + j >= G, block + j <= n_seq * blocks - 1)
            shifts.append(lse + hidden(okay))
        dk, dv, more = pair_grads(kv_ext[0, win, :], kv_ext[1, win, :], shifts, q, g, delta, scaling)
        acc[0, win, :] += dk
        acc[1, win, :] += dv
        dq_acc[b] = dq + more

    def found(part, b):
        return jnp.concatenate([rand[part][pos[b * RND + j]] for j in range(RND)], axis=0)

    def far_values(i):
        b = block_at(i)
        q, g, lse, _ = operands(b)
        block = seq * blocks + b
        scores = dot(found(0, b), q, 1, 1) * (scaling * LOG2E)
        parts = []
        for j in range(RND):
            other = owner[j, block] * blocks + slot[j, block]
            okay = jnp.logical_and(other >= G, jnp.abs(other - block) >= 2)
            shift = lse + hidden(okay)
            parts.append(jnp.exp2(scores[j * BLK : (j + 1) * BLK] - shift).astype(BF16))
        weights = jnp.concatenate(parts, axis=0)
        far_weights[b] = weights
        dv = dot(weights, g, 1, 0)
        for j in range(RND):
            rpart[1, b * RND + j] = dv[j * BLK : (j + 1) * BLK].astype(BF16)

    def far_keys(i):
        b = block_at(i)
        q, g, _, delta = operands(b)
        at = pl.multiple_of(b * BLK, BLK)
        rise = dot(found(1, b), g, 1, 1) - delta
        score_grad = (far_weights[b].astype(F32) * rise).astype(BF16)
        dk = dot(score_grad, q, 1, 0) * scaling
        for j in range(RND):
            rpart[0, b * RND + j] = dk[j * BLK : (j + 1) * BLK].astype(BF16)
        total = dq_acc[b] + dot(found(0, b), score_grad, 0, 0)
        dq_all[pl.ds(at, BLK)] = (total.T * (scaling * LIFT)).astype(BF16).reshape(BLK, group, HD)

    last = pieces - 1
    early = sum(stage < last for stage, _ in plan)
    firsts = {}
    for i, (stage, _) in enumerate(plan):
        for s in range(stage + 1):
            firsts.setdefault(s, i)

    def near_early(i):
        for s in range(last):
            if s in firsts and firsts[s] < early:
                @pl.when(i == firsts[s])
                def _():
                    landed(s)

        near(i)

    loop(0, early, near_early)
    for s in range(last):
        if s not in firsts or firsts[s] >= early:
            landed(s)
    loop(1, n_seq, lambda d: rand_copy(0, d).wait())
    loop(0, early, far_values)
    landed(last)
    loop(early, blocks, far_values)
    loop(1, n_seq, lambda d: rand_copy(1, d).wait_send())

    def back_copy(part, d):
        peer = lax.rem(seq + d, n_seq)
        return remote(
            picked.at[part, slots_of(peer)], rback.at[part, slots_of(seq)],
            rs.at[part, d], rr.at[part, d], seq=peer,
        )

    def gather(part):
        def move(i):
            picked[part, i] = rpart[part, back[i]]

        loop(0, n_seq * most, move)

    gather(1)
    loop(1, n_seq, lambda d: back_copy(1, d).start())
    loop(early, blocks, near)

    halo_part[0] = acc[:, 0:BLK, :].astype(BF16)
    halo_part[1] = acc[:, BLK + span :, :].astype(BF16)
    gpart[...] = gacc[...].astype(BF16)

    def dq_copy(d):
        peer = partner(d)
        src = dq_all.at[pl.ds(pl.multiple_of(peer * toks, toks), toks)]
        return remote(src, heads_of(dq_out, head), ds.at[d], dr.at[d], head=peer)

    def kv_copy(part, d):
        peer = partner(d)
        src = kv_sum.at[part, pl.ds(pl.multiple_of(peer * toks, 32), toks), :]
        return remote(src, kv_out.at[head, part], es.at[part, d], er.at[part, d], head=peer)

    def part_copy():
        return remote(gpart, gall.at[seq], ps.at[0], pr.at[seq], seq=lax.rem(seq, 2))

    down_grad = remote(halo_part.at[0], halo.at[0], hs.at[0], hr.at[0], seq=down)
    up_grad = remote(halo_part.at[1], halo.at[1], hs.at[1], hr.at[1], seq=up)
    down_grad.start()
    up_grad.start()

    @pl.when(seq > 1)
    def _():
        part_copy().start()

    loop(1, n_seq, lambda d: rand_copy(1, d).wait_recv())
    loop(0, blocks, far_keys)
    gather(0)
    loop(1, n_seq, lambda d: back_copy(0, d).start())
    own_dq = pltpu.make_async_copy(dq_all.at[here], heads_of(dq_out, head), ls.at[5])
    for d in sends:
        dq_copy(d).start()
    own_dq.start()
    for part in range(2):
        rback[part, slots_of(seq)] = picked[part, slots_of(seq)]

    for d in range(1, n_head):
        for kind in range(2):
            kv_head(kind, d).wait_send()
            line_head(kind, d).wait_send()
            for i in range(pieces):
                piece_send(kind, d, i).wait_send()

    def absorb(part, d):
        base = lax.rem(seq + n_seq - d, n_seq) * most

        def block_sum(block):
            over = pl.ds(pl.multiple_of(block * BLK + BLK, BLK), BLK)
            value = acc[part, over, :]
            for m in range(most):
                share = jnp.where(pick[base + m] == block, 1.0, 0.0).astype(F32)
                value = value + share * rback[part, base + m].astype(F32)
            acc[part, over, :] = value

        loop(0, blocks, block_sum)

    absorb(1, 0)
    absorb(0, 0)

    @pl.when(seq == 0)
    def _():
        for part in range(2):
            loop(1, n_seq, lambda d: glob_copy(part, d).wait_send())

    def finish(part):
        for d in range(1, n_head):
            kv_copy(part, d).wait()
        whole = jnp.concatenate([kv_out[p, part] for p in range(n_head)], axis=1).astype(F32)
        (dk_out, dv_out)[part][...] = (whole * LIFT).reshape(toks, n_head, HD).astype(BF16)

    for part in (1, 0):
        def take(d):
            back_copy(part, d).wait()
            absorb(part, d)

        loop(1, n_seq, take)
        if part:
            passed = remote(gpart, gall.at[1], ps.at[0], pr.at[1], seq=0)

            def add(d):
                remote(gpart, gall.at[d], ps.at[0], pr.at[d], seq=0).wait_recv()
                gacc[...] += gall[d].astype(F32)

            @pl.when(seq == 1)
            def _():
                loop(1, n_seq // 2, lambda i: add(2 * i + 1))
                gpart[...] = gacc[...].astype(BF16)
                passed.start()
                passed.wait_send()

            @pl.when(seq == 0)
            def _():
                loop(1, (n_seq + 1) // 2, lambda i: add(2 * i))
                add(1)
                acc[:, BLK : BLK + G * BLK, :] += gacc[...]

            @pl.when(seq > 1)
            def _():
                part_copy().wait_send()

            down_grad.wait()
            up_grad.wait()
            acc[:, BLK : 2 * BLK, :] += halo[1].astype(F32)
            acc[:, span : span + BLK, :] += halo[0].astype(F32)
        kv_sum[part] = acc[part, BLK : BLK + span, :].astype(BF16)
        for d in sends:
            kv_copy(part, d).start()
        kv_out[head, part] = kv_sum[part, pl.ds(pl.multiple_of(head * toks, 32), toks), :]
        if part == 0:
            own_dq.wait()
            for d in range(1, n_head):
                dq_copy(d).wait()
            finish(1)
            finish(0)


def per_device(
    n_seq, n_head,
    queries, key_states, value_states, outputs, output_grad, logsumexp, random_owner, random_slot,
):
    toks, heads, _ = queries.shape
    group = heads // n_head
    rows = toks * group
    span = toks * n_head
    blocks = span // BLK
    per_row = blocks * RND
    most = max(1, (per_row + n_seq - 1) // n_seq)
    pieces = 3 if toks % 3 == 0 else 1
    vmem = pl.BlockSpec(memory_space=pltpu.VMEM)
    smem = pl.BlockSpec(memory_space=pltpu.SMEM)
    hbm = pl.BlockSpec(memory_space=pl.ANY)
    dma = pltpu.SemaphoreType.DMA

    slots = n_seq * most
    step = BLK * group
    grads = pl.pallas_call(
        functools.partial(fused, n_seq, n_head, most, blocks, pieces),
        out_shape=[
            jax.ShapeDtypeStruct((toks, heads, HD), BF16),
            jax.ShapeDtypeStruct((toks, n_head, HD), BF16),
            jax.ShapeDtypeStruct((toks, n_head, HD), BF16),
        ],
        in_specs=[smem, smem, hbm, hbm, hbm, vmem, vmem, vmem],
        out_specs=[hbm, vmem, vmem],
        scratch_shapes=[
            pltpu.VMEM((n_head, 2, toks, HD), BF16),
            pltpu.VMEM((n_head, 2, toks, HD), BF16),
            pltpu.VMEM((n_head, rows // 128, 1, 128), F32),
            pltpu.SMEM((slots,), jnp.int32),
            pltpu.SMEM((per_row,), jnp.int32),
            pltpu.SMEM((slots,), jnp.int32),
            pltpu.VMEM((blocks, RND * BLK, step), BF16),
            pltpu.VMEM((n_head, toks, group, HD), BF16),
            pltpu.VMEM((n_head, toks, group, HD), BF16),
            pltpu.VMEM((n_head, rows // 128, 1, 128), F32),
            pltpu.VMEM((span, group, HD), BF16),
            pltpu.VMEM((span, group, HD), BF16),
            pltpu.VMEM((n_head * rows // 128, 1, 128), F32),
            pltpu.VMEM((n_head * rows // 128, 1, 128), F32),
            pltpu.VMEM((2, span + 2 * BLK, HD), BF16),
            pltpu.VMEM((2, G * BLK, HD), BF16),
            pltpu.VMEM((slots, BLK, HD), BF16),
            pltpu.VMEM((slots, BLK, HD), BF16),
            pltpu.VMEM((2, slots, BLK, HD), BF16),
            pltpu.VMEM((2, blocks, BLK, HD), BF16),
            pltpu.VMEM((2, span + 2 * BLK, HD), F32),
            pltpu.VMEM((2, G * BLK, HD), F32),
            pltpu.VMEM((blocks, HD, step), F32),
            pltpu.VMEM((span, group, HD), BF16),
            pltpu.VMEM((2, per_row, BLK, HD), BF16),
            pltpu.VMEM((2, slots, BLK, HD), BF16),
            pltpu.VMEM((2, 2, BLK, HD), BF16),
            pltpu.VMEM((2, 2, BLK, HD), BF16),
            pltpu.VMEM((2, G * BLK, HD), BF16),
            pltpu.VMEM((n_seq, 2, G * BLK, HD), BF16),
            pltpu.VMEM((2, span, HD), BF16),
            dma((6,)), dma((2, n_head)), dma((2, n_head)), dma((2, n_head)),
            dma((2, n_head)), dma((2, n_head)),
            dma((2, n_head, pieces)), dma((2, n_head, pieces)),
            dma((n_head,)), dma((n_head,)), dma((2, n_head)), dma((2, n_head)),
            dma((2, n_seq)), dma((2, n_seq)), dma((2, 2)), dma((2, 2)), dma((2,)), dma((2,)),
            dma((2, n_seq)), dma((2,)), dma((1,)), dma((n_seq,)),
            dma((2, n_seq)), dma((2, n_seq)),
        ],
        compiler_params=pltpu.CompilerParams(
            collective_id=0, has_side_effects=True, vmem_limit_bytes=60 << 20
        ),
        name="fused",
    )(
        random_owner.T, random_slot.T, queries, output_grad, outputs,
        key_states, value_states, logsumexp.T,
    )
    return tuple(grad * jnp.asarray(1.0 / LIFT, BF16) for grad in grads)


def solution(mesh):
    wide = P(("seq", "head"), None, None)
    return jax.shard_map(
        functools.partial(per_device, mesh.shape["seq"], mesh.shape["head"]),
        mesh=mesh,
        in_specs=(wide, wide, wide, wide, wide, P(("seq", "head"), None), P(), P()),
        out_specs=(wide, wide, wide),
        check_vma=False,
    )
```
